32 devices in a mesh: seq: 4 (over y, x), fsdp: 8 (over z, core).
Axes of the slice: x: 2, y: 2, z: 4, core: 2. Of those that a mesh axis runs over, the one named last changes fastest.
Arguments:
- frames: bfloat16 [8, 2048, 1536], P('fsdp', 'seq'), may hold values from -6 to 6
- lengths: int32 [8], P('fsdp'), may hold values from 512 to 2048, as said below
- gain: float32 [1536], replicated, may hold values from 0.5 to 1.5
- w_pointwise: bfloat16 [1536, 3072], P('fsdp'), may hold values from -0.15625 to 0.15625
- w_depthwise: float32 [31, 1536], replicated, may hold values from -1 to 1
- w_output: bfloat16 [1536, 1536], P('fsdp'), may hold values from -0.15625 to 0.15625
- cotangent: bfloat16 [8, 2048, 1536], P('fsdp', 'seq'), may hold values from -6 to 6
Outputs:
- output: bfloat16 [8, 2048, 1536], P('fsdp', 'seq')
- grad_frames: bfloat16 [8, 2048, 1536], P('fsdp', 'seq')
- grad_pointwise: float32 [1536, 3072], P('fsdp')
- grad_output: float32 [1536, 1536], P('fsdp')
- grad_gain: float32 [1536], replicated
- grad_depthwise: float32 [31, 1536], replicated
The draws below stay inside these ranges and needn't reach their ends.
Inputs may be any that keep to these rules, and one draw needn't show every extreme that they name: `lengths`: the first utterance fills all 2048 slots.
All inputs are finite; a program needn't handle non-finite values.
Results may differ from the reference program's by a relative error of at most 0.014.
Values may be sent and summed in bfloat16 or wider, within the bound.
No kernel may reach another device: no remote copies, remote signals or barrier semaphores. Data moves between devices by JAX's collectives and lax.ppermute only.
A program may use at most 128 MiB of HBM per device.

```python
import jax
import jax.numpy as jnp
from jax import lax

D = 1536
KERNEL = 31
F = 512
B = 8
S = 2048
N_SEQ = 4


def draw_lengths(key, part):
    drawn = jax.random.randint(key, (B,), S // 4, S + 1).astype(jnp.int32)
    return drawn.at[0].set(S)


def level_of(key, dims, shards, low, largest):
    loudness = 1.0
    for dim, parts in shards:
        heights = jax.random.uniform(jax.random.fold_in(jax.random.fold_in(key, 6), dim), (parts,), jnp.float32, low / len(shards), largest / len(shards))
        loudness = loudness * jnp.repeat(jnp.exp(heights), dims[dim] // parts).reshape((-1,) + (1,) * (len(dims) - 1 - dim))
    return loudness


def centred(rng, extent, scale, limit, shards=(), kind=jnp.bfloat16):
    values = scale * jax.random.normal(rng, extent, jnp.float32)
    if shards:
        values = values * level_of(rng, extent, shards, -0.22, 0.18)
    return jnp.clip(values, -limit, limit).astype(kind)


def setup_inputs(seed: int = 0) -> dict:
    splits = jax.random.split(jax.random.key(seed), 8)
    return {
        "frames": centred(splits[0], (B, S, D), 1.0, 6.0, ((0, 8), (1, 4))),
        "lengths": draw_lengths(jax.random.fold_in(splits[7], 71), 0),
        "gain": jnp.clip(1.0 + 0.1 * jax.random.normal(splits[2], (D,), jnp.float32), 0.5, 1.5),
        "w_pointwise": centred(splits[3], (D, 2 * D), D ** -0.5, 0.15625, ((0, 8),)),
        "w_depthwise": centred(splits[4], (KERNEL, D), KERNEL ** -0.5, 1.0, (), jnp.float32),
        "w_output": centred(splits[5], (D, D), D ** -0.5, 0.15625, ((0, 8),)),
        "cotangent": centred(splits[6], (B, S, D), 1.0, 6.0, ((0, 8), (1, 4))),
    }


EPS = 1e-05

def reference(frames, lengths, gain, w_pointwise, w_depthwise, w_output, cotangent):
    half_width = (KERNEL - 1) // 2
    as_float = frames.astype(jnp.float32)
    center = lax.optimization_barrier(jnp.mean(as_float, axis=-1, keepdims=True))
    spread = lax.optimization_barrier(jnp.mean((as_float - center) ** 2, axis=-1, keepdims=True))
    inverse = lax.rsqrt(spread + EPS)
    normed = (as_float - center) * inverse
    lifted = (normed * gain).astype(jnp.bfloat16)
    mask = (jnp.arange(S, dtype=jnp.int32)[None, :] < lengths[:, None]).astype(jnp.float32)[..., None]
    joined = jnp.dot(lifted.reshape(B * S, D), w_pointwise, preferred_element_type=jnp.float32).reshape(B, S, 2 * D)
    value = joined[..., :D]
    gate_sig = jax.nn.sigmoid(joined[..., D:])
    glu = (value * gate_sig * mask).astype(jnp.bfloat16)
    glu_pad = jnp.pad(glu.astype(jnp.float32), ((0, 0), (half_width, half_width), (0, 0)))
    conv = jnp.zeros((B, S, D), jnp.float32)
    for offset in range(KERNEL):
        conv = conv + w_depthwise[offset] * glu_pad[:, offset:offset + S]
    conv_sig = jax.nn.sigmoid(conv)
    swished = (conv * conv_sig).astype(jnp.bfloat16)
    branch = jnp.dot(swished.reshape(B * S, D), w_output, preferred_element_type=jnp.float32).reshape(B, S, D)
    output = (as_float + branch).astype(jnp.bfloat16)
    branch_grad = (cotangent.astype(jnp.float32) * mask).astype(jnp.bfloat16)
    swish_grad = jnp.dot(branch_grad.reshape(B * S, D), w_output.T, preferred_element_type=jnp.float32).reshape(B, S, D)
    conv_grad = (swish_grad * conv_sig * (1.0 + conv * (1.0 - conv_sig))).astype(jnp.bfloat16)
    grad_pad = jnp.pad(conv_grad.astype(jnp.float32), ((0, 0), (half_width, half_width), (0, 0)))
    glu_grad = jnp.zeros((B, S, D), jnp.float32)
    tap_rows = []
    for offset in range(KERNEL):
        back = KERNEL - 1 - offset
        glu_grad = glu_grad + w_depthwise[offset] * grad_pad[:, back:back + S]
        tap_rows.append(lax.optimization_barrier(jnp.sum(conv_grad.astype(jnp.float32) * glu_pad[:, offset:offset + S], axis=(0, 1))))
    grad_depthwise = jnp.stack(tap_rows, axis=0)
    glu_grad = glu_grad * mask
    joined_grad = jnp.concatenate([glu_grad * gate_sig, glu_grad * value * gate_sig * (1.0 - gate_sig)], axis=-1).astype(jnp.bfloat16)
    blocks = B * N_SEQ

    def add_terms(carry, pieces):
        lifted_b, joined_b, swished_b, branch_b = pieces
        first = jnp.dot(lifted_b.T, joined_b, preferred_element_type=jnp.float32).astype(jnp.bfloat16)
        second = jnp.dot(swished_b.T, branch_b, preferred_element_type=jnp.float32).astype(jnp.bfloat16)
        first = lax.optimization_barrier(first)
        second = lax.optimization_barrier(second)
        return ((carry[0] + first.astype(jnp.float32), carry[1] + second.astype(jnp.float32)), None)
    start = (jnp.zeros((D, 2 * D), jnp.float32), jnp.zeros((D, D), jnp.float32))
    (grad_pointwise, grad_output), _ = lax.scan(add_terms, start, (lifted.reshape(blocks, F, D), joined_grad.reshape(blocks, F, 2 * D), swished.reshape(blocks, F, D), branch_grad.reshape(blocks, F, D)))
    lifted_grad = jnp.dot(joined_grad.reshape(B * S, 2 * D), w_pointwise.T, preferred_element_type=jnp.float32).reshape(B, S, D)
    grad_gain = lax.optimization_barrier(jnp.sum(lifted_grad * normed, axis=(0, 1)))
    scaled = lifted_grad * gain
    norm_grad = inverse * (scaled - lax.optimization_barrier(jnp.mean(scaled, axis=-1, keepdims=True)) - normed * lax.optimization_barrier(jnp.mean(scaled * normed, axis=-1, keepdims=True)))
    grad_frames = (cotangent.astype(jnp.float32) + norm_grad).astype(jnp.bfloat16)
    return (output, grad_frames, grad_pointwise, grad_output, grad_gain, grad_depthwise)
```

```python
import functools

import jax
import jax.numpy as jnp
from jax import lax
from jax.experimental import pallas as pl
from jax.experimental.pallas import tpu as pltpu
from jax.sharding import PartitionSpec as P

EPS = 1e-05
BF = jnp.bfloat16
F32 = jnp.float32
BOTH = ("seq", "fsdp")
N_SEQ, N_Z, N_CORE = 4, 4, 2
VMEM_LIMIT = 60 * 1024 * 1024


def device_pairs(move):
    def flat(s, z, c):
        return (s * N_Z + z) * N_CORE + c
    return [
        (flat(s, z, c), flat(*move(s, z, c)))
        for s in range(N_SEQ) for z in range(N_Z) for c in range(N_CORE)
    ]


ACROSS = {
    "core": device_pairs(lambda s, z, c: (s, z, 1 - c)),
    "x": device_pairs(lambda s, z, c: (s ^ 1, z, c)),
    "y": device_pairs(lambda s, z, c: (s ^ 2, z, c)),
    "d": device_pairs(lambda s, z, c: (s ^ 3, z, c)),
    "z1": device_pairs(lambda s, z, c: (s, (z + 1) % N_Z, c)),
    "z2": device_pairs(lambda s, z, c: (s, (z + 2) % N_Z, c)),
    "z3": device_pairs(lambda s, z, c: (s, (z + 3) % N_Z, c)),
}


def send(block, way):
    return lax.ppermute(block, BOTH, ACROSS[way])


def part(block, index, size, axis):
    return lax.dynamic_slice_in_dim(block, index * size, size, axis)


def hint(bytes_accessed=1024):
    return pl.CostEstimate(flops=0, bytes_accessed=bytes_accessed, transcendentals=0)


def joined_kernel(j, behind, first_call, where_ref, lifted_ref, *refs):
    own, came = refs[0:2], refs[2:4]
    count = 2 if j == 3 else 1
    mine, other = refs[4:4 + count], refs[4 + count:4 + 2 * count]
    w_value_ref, w_gate_ref, value_ref, sig_ref, glu_ref = refs[-5:]
    z, c, valid = where_ref[1], where_ref[2], where_ref[3]
    rows = own[0].shape[0]
    outs = w_value_ref, w_gate_ref
    for source, pieces, core in ((own, mine, c), (came, other, 1 - c)):
        at = pl.multiple_of((z * N_CORE + core) * rows, 64)
        for side in range(2):
            outs[side][pl.ds(at, rows), :] = source[side][...]
        for index, k in enumerate(behind):
            at = (lax.rem(z + N_Z - k, N_Z) * N_CORE + core) * rows
            part_rows = rows // count
            for n in range(count):
                low = pl.ds(pl.multiple_of(at + n * part_rows, 32), part_rows)
                for side in range(2):
                    outs[side][low, :] = pieces[n][index, side]
    value = jnp.dot(lifted_ref[...], w_value_ref[...], preferred_element_type=F32)
    value_ref[...] = value
    sig = jax.nn.sigmoid(jnp.dot(lifted_ref[...], w_gate_ref[...], preferred_element_type=F32))
    sig_ref[...] = sig
    position = lax.broadcasted_iota(jnp.int32, sig.shape, 0)
    glu_ref[...] = jnp.where(position < valid, value * sig, 0.0).astype(BF)


def joined_call(j, behind, where, lifted, w_own, w_came, mine, other, buffers):
    frames, width = lifted.shape
    block = width // N_SEQ
    rows = w_own.shape[0]
    whole = lambda a: pl.BlockSpec(a.shape, lambda i, at: (0,) * a.ndim)
    column = lambda n: pl.BlockSpec((n, block), lambda i, at: (0, at[0] ^ j))
    second = pl.BlockSpec((rows, block), lambda i, at: (0, N_SEQ + (at[0] ^ j)))
    operands = [lifted, w_own, w_own, w_came, w_came, *mine, *other]
    specs = [whole(lifted), column(rows), second, column(rows), second]
    specs += [whole(a) for a in (*mine, *other)]
    aliases = {}
    if buffers:
        aliases = {1 + len(operands) + n: n for n in range(5)}
        operands += buffers
        specs += [pl.BlockSpec(memory_space=pl.ANY)] * 5
    return pl.pallas_call(
        functools.partial(joined_kernel, j, behind, not buffers),
        grid_spec=pltpu.PrefetchScalarGridSpec(
            num_scalar_prefetch=1, grid=(1,), in_specs=specs,
            out_specs=[column(width), column(width), column(frames), column(frames), column(frames)],
        ),
        out_shape=[
            jax.ShapeDtypeStruct((width, width), BF), jax.ShapeDtypeStruct((width, width), BF),
            jax.ShapeDtypeStruct((frames, width), F32), jax.ShapeDtypeStruct((frames, width), F32),
            jax.ShapeDtypeStruct((frames, width), BF),
        ],
        input_output_aliases=aliases,
        compiler_params=pltpu.CompilerParams(vmem_limit_bytes=VMEM_LIMIT),
        cost_estimate=hint(),
        name="joined_%d" % j,
    )(where, *operands)


EDGE = 16
LANES = 128
SUB = 8


def extend(ext_ref, low, body, high):
    count = body.shape[0]
    ext_ref[0:EDGE, :] = low.astype(F32)
    ext_ref[EDGE:EDGE + count, :] = body.astype(F32)
    ext_ref[EDGE + count:, :] = high.astype(F32)


def tap_sum(ext_ref, wide, first, height, order):
    total = None
    for o, k in enumerate(order):
        rows = ext_ref[pl.ds(first + (o + 1), height), :]
        term = rows.reshape(height // SUB, SUB, LANES) * wide[k][None]
        total = term if total is None else total + term
    return total.reshape(height, LANES)


def widened(taps_ref, lanes):
    return [jnp.broadcast_to(taps_ref[k:k + 1, lanes], (SUB, LANES)) for k in range(taps_ref.shape[0])]


def forward_kernel(glu_ref, low_ref, high_ref, taps_ref, swished_ref, slope_ref, ext_ref):
    frames, width = glu_ref.shape
    height = 64

    @pl.loop(0, width // LANES)
    def _(b):
        lanes = pl.ds(pl.multiple_of(b * LANES, LANES), LANES)
        wide = widened(taps_ref, lanes)
        extend(ext_ref, low_ref[:, lanes], glu_ref[:, lanes], high_ref[:, lanes])

        @pl.loop(0, frames // height)
        def _(i):
            first = pl.multiple_of(i * height, height)
            conv = tap_sum(ext_ref, wide, first, height, range(len(wide)))
            sig = jax.nn.sigmoid(conv)
            at = pl.ds(first, height)
            swished_ref[at, lanes] = (conv * sig).astype(BF)
            slope_ref[at, lanes] = sig * (1.0 + conv * (1.0 - sig))


def forward_call(glu, low, high, taps):
    frames, width = glu.shape
    size = width // N_SEQ
    column = lambda rows: pl.BlockSpec((rows, size), lambda i: (0, i))
    return pl.pallas_call(
        forward_kernel,
        grid=(width // size,),
        out_shape=(jax.ShapeDtypeStruct((frames, width), BF), jax.ShapeDtypeStruct((frames, width), F32)),
        in_specs=[column(frames), column(EDGE), column(EDGE), column(taps.shape[0])],
        out_specs=(column(frames),) * 2,
        scratch_shapes=[pltpu.VMEM((frames + 2 * EDGE, LANES), F32)],
        compiler_params=pltpu.CompilerParams(vmem_limit_bytes=VMEM_LIMIT),
        cost_estimate=hint(),
        name="conv_forward",
    )(glu, low, high, taps)


def backward_kernel(
    where_ref, grad_ref, grad_low_ref, grad_high_ref, glu_ref, low_ref, high_ref, taps_ref, value_ref, sig_ref, *refs
):
    mine_ref, send_ref, value_grad_ref, gate_grad_ref, tap_grad_ref, ext_ref, sum_ref = refs[-7:]
    frames, width = glu_ref.shape
    taps = taps_ref.shape[0]
    height = 64
    c, valid = where_ref[2], where_ref[3]

    @pl.loop(0, width // LANES)
    def _(b):
        lanes = pl.ds(pl.multiple_of(b * LANES, LANES), LANES)
        wide = widened(taps_ref, lanes)
        extend(ext_ref, grad_low_ref[:, lanes], grad_ref[:, lanes], grad_high_ref[:, lanes])

        @pl.loop(0, frames // height)
        def _(i):
            first = pl.multiple_of(i * height, height)
            at = pl.ds(first, height)
            glu_grad = tap_sum(ext_ref, wide, first, height, range(taps - 1, -1, -1))
            position = first + lax.broadcasted_iota(jnp.int32, (height, LANES), 0)
            sig = sig_ref[at, lanes]
            scaled = jnp.where(position < valid, glu_grad, 0.0) * sig
            by_gate = (scaled * value_ref[at, lanes] * (1.0 - sig)).astype(BF)
            scaled = scaled.astype(BF)
            value_grad_ref[at, lanes] = scaled
            gate_grad_ref[at, lanes] = by_gate
            mine_ref[at, lanes] = jnp.where(c == 0, scaled, by_gate)
            send_ref[at, lanes] = jnp.where(c == 0, by_gate, scaled)

        extend(ext_ref, low_ref[:, lanes], glu_ref[:, lanes], high_ref[:, lanes])
        sum_ref[...] = jnp.zeros_like(sum_ref)

        @pl.loop(0, frames // height)
        def _(i):
            first = pl.multiple_of(i * height, height)
            grad = grad_ref[pl.ds(first, height), lanes].astype(F32)
            for k in range(taps):
                term = grad * ext_ref[pl.ds(first + (k + 1), height), :]
                sum_ref[k] += jnp.sum(term.reshape(height // SUB, SUB, LANES), axis=0)

        tap_grad_ref[:, lanes] = jnp.sum(sum_ref[...], axis=1)


def backward_call(j, where, grad, grad_low, grad_high, glu, low, high, taps, value, sig, buffers):
    frames, width = glu.shape
    size = width // N_SEQ
    count = taps.shape[0]
    column = lambda rows: pl.BlockSpec((rows, size), lambda i, at: (0, at[0] ^ j))
    alone = pl.BlockSpec((frames, size), lambda i, at: (0, 0))
    operands = [grad, grad_low, grad_high, glu, low, high, taps, value, sig]
    specs = [column(n) for n in (frames, EDGE, EDGE, frames, EDGE, EDGE, count, frames, frames)]
    aliases = {}
    if buffers:
        aliases = {1 + len(operands) + n: 2 + n for n in range(3)}
        operands += buffers
        specs += [pl.BlockSpec(memory_space=pl.ANY)] * 3
    small = jax.ShapeDtypeStruct((frames, size), BF)
    full = jax.ShapeDtypeStruct((frames, width), BF)
    mine, sent, *buffers = pl.pallas_call(
        backward_kernel,
        grid_spec=pltpu.PrefetchScalarGridSpec(
            num_scalar_prefetch=1, grid=(1,), in_specs=specs,
            out_specs=[alone, alone, column(frames), column(frames), column(count + 1)],
            scratch_shapes=[
                pltpu.VMEM((frames + 2 * EDGE, LANES), F32), pltpu.VMEM((count + 1, SUB, LANES), F32),
            ],
        ),
        out_shape=[small, small, full, full, jax.ShapeDtypeStruct((count + 1, width), F32)],
        input_output_aliases=aliases,
        compiler_params=pltpu.CompilerParams(vmem_limit_bytes=VMEM_LIMIT),
        cost_estimate=hint(),
        name="conv_backward_%d" % j,
    )(where, *operands)
    return mine, sent, buffers


def edges(block):
    count = lax.axis_size("seq")
    forward = [(i, i + 1) for i in range(count - 1)]
    backward = [(target, source) for source, target in forward]
    return (
        lax.ppermute(block[block.shape[0] - EDGE:], "seq", forward),
        lax.ppermute(block[:EDGE], "seq", backward),
    )


def transposed_dot(left, right):
    return lax.dot_general(left, right, (((0,), (0,)), ((), ())), preferred_element_type=F32)


def final_kernel(block, where_ref, *refs):
    pieces, (pointwise_ref, output_ref) = refs[:-2], refs[-2:]
    s = where_ref[0]
    width = N_SEQ * block
    for j in range(N_SEQ):
        for side in range(2):
            at = pl.multiple_of(side * width + (s ^ j) * block, 128)
            pointwise_ref[:, pl.ds(at, block)] = pieces[j][side].astype(F32)
        rows = pieces[N_SEQ + j].shape[0]
        output_ref[pl.ds(pl.multiple_of((s ^ j) * rows, 16), rows), :] = pieces[N_SEQ + j][...].astype(F32)


def final_call(where, block, pointwise_pieces, output_pieces):
    width = N_SEQ * block
    rows = pointwise_pieces[0].shape[1]
    vmem = pl.BlockSpec(memory_space=pltpu.VMEM)
    operands = (*pointwise_pieces, *output_pieces)
    return pl.pallas_call(
        functools.partial(final_kernel, block),
        out_shape=(
            jax.ShapeDtypeStruct((rows, 2 * width), F32),
            jax.ShapeDtypeStruct((rows, width), F32),
        ),
        in_specs=[pl.BlockSpec(memory_space=pltpu.SMEM)] + [vmem] * len(operands),
        out_specs=(vmem, vmem),
        compiler_params=pltpu.CompilerParams(vmem_limit_bytes=VMEM_LIMIT),
        cost_estimate=hint(),
        name="final",
    )(where, *operands)


def after(values, *first):
    return lax.optimization_barrier((values, first))[0]


def on_slice(frames, lengths, gain, w_pointwise, w_depthwise, w_output, cotangent):
    frame_count, width = frames.shape[1:]
    taps = w_depthwise.shape[0]
    block = width // N_SEQ
    rows = width // (N_Z * N_CORE)
    s = lax.axis_index("seq")
    z, c = lax.axis_index("fsdp") // N_CORE, lax.axis_index("fsdp") % N_CORE
    where = jnp.stack([s, z, c, lengths[0] - s * frame_count]).astype(jnp.int32)

    first = jnp.stack([
        lax.dynamic_slice_in_dim(w_pointwise, s * block, block, 1),
        lax.dynamic_slice_in_dim(w_pointwise, width + s * block, block, 1),
    ])
    behind = (1, 3, 2)
    group = [send(first, "z%d" % k) for k in behind]
    w_came = send(w_pointwise, "core")
    as_float = frames[0].astype(F32)
    center = jnp.mean(as_float, axis=-1, keepdims=True)
    spread = jnp.mean((as_float - center) ** 2, axis=-1, keepdims=True)
    inverse = lax.rsqrt(spread + EPS)
    normed = (as_float - center) * inverse
    lifted = (normed * gain).astype(BF)
    position = jnp.arange(frame_count, dtype=jnp.int32)
    mask = (position < where[3]).astype(F32)[:, None]
    branch_grad = (cotangent[0].astype(F32) * mask).astype(BF)
    group, lifted, branch_grad, w_came = lax.optimization_barrier(
        (jnp.stack(group), lifted, branch_grad, w_came)
    )
    full_output = lax.all_gather(after(w_output, group), "fsdp", axis=0, tiled=True)

    from_x, from_y = send(group, "x"), send(group, "y")
    lifted_other = send(lifted, "core")
    group_other = send(group, "core")
    turned, turned_other = lifted.T, lifted_other.T
    from_x, from_y, turned, turned_other, group_other = lax.optimization_barrier(
        (from_x, from_y, turned, turned_other, group_other)
    )
    top, bottom = send(from_x[:, :, :rows // 2], "y"), send(from_y[:, :, rows // 2:], "x")
    from_x_other, from_y_other = send(from_x, "core"), send(from_y, "core")
    buffers = []
    for j, mine, other in ((0, group, group_other), (1, from_x, from_x_other), (2, from_y, from_y_other)):
        buffers = joined_call(j, behind, where, lifted, w_pointwise, w_came, [mine], [other], buffers)
    top, bottom, buffers = lax.optimization_barrier((top, bottom, buffers))
    top_other, bottom_other = send(top, "core"), send(bottom, "core")
    buffers = joined_call(
        3, behind, where, lifted, w_pointwise, w_came, [top, bottom], [top_other, bottom_other], buffers
    )
    w_value, w_gate, value, gate_sig, glu = buffers

    glu_low, glu_high = edges(glu)
    swished, slope = forward_call(glu, glu_low, glu_high, w_depthwise)
    contract = (((1,), (1,)), ((), ()))
    swish_grad = lax.dot_general(branch_grad, full_output, contract, preferred_element_type=F32)
    conv_grad = (swish_grad * slope).astype(BF)
    grad_low, grad_high = edges(conv_grad)
    term_output = transposed_dot(after(swished, conv_grad), branch_grad).astype(BF)
    grad_low, grad_high, term_output = lax.optimization_barrier((grad_low, grad_high, term_output))
    owned_output = lax.psum_scatter(term_output, "fsdp", scatter_dimension=0, tiled=True)
    branch = jnp.dot(swished, full_output, preferred_element_type=F32)
    output = (as_float + branch).astype(BF)

    buffers, terms, came = [], {}, {}
    waits = {2: 3, 0: 1}
    for j, way in ((3, "d"), (1, "x"), (2, "y"), (0, None)):
        if j in waits:
            buffers = after(buffers, terms[waits[j]])
        mine, sent, buffers = backward_call(
            j, where, conv_grad, grad_low, grad_high, glu, glu_low, glu_high, w_depthwise, value, gate_sig, buffers
        )
        other = send(sent, "core")
        term = jnp.dot(turned, mine, preferred_element_type=F32) + jnp.dot(
            turned_other, other, preferred_element_type=F32
        )
        terms[j] = term.astype(BF) if j else term
        if way:
            came[j] = send(terms[j], way)
    grad_value, grad_gate, tap_grad = buffers

    grad_value, grad_gate = after((grad_value, grad_gate), terms[2])
    lifted_grad = lax.dot_general(
        grad_value, w_value, contract, preferred_element_type=F32
    ) + lax.dot_general(grad_gate, w_gate, contract, preferred_element_type=F32)
    gain_term = jnp.sum(lifted_grad * normed, axis=0)
    small = jnp.concatenate([tap_grad[:taps], gain_term[None]], axis=0)

    total = (terms[0] + came[1].astype(F32) + came[2].astype(F32) + came[3].astype(F32)).astype(BF)
    total, small, lifted_grad, owned_output = lax.optimization_barrier((total, small, lifted_grad, owned_output))
    own = part(total, z, 2 * rows, 0)
    over_z = [send(part(total, (z + k) % N_Z, 2 * rows, 0), "z%d" % k) for k in (2, 1, 3)]
    scaled = lifted_grad * gain
    norm_grad = inverse * (
        scaled
        - jnp.mean(scaled, axis=-1, keepdims=True)
        - normed * jnp.mean(scaled * normed, axis=-1, keepdims=True)
    )
    grad_frames = (cotangent[0].astype(F32) + norm_grad).astype(BF)
    quarter = rows // N_SEQ
    own_output = part(owned_output, s, quarter, 0).astype(F32)
    for j, way in ((3, "d"), (1, "x"), (2, "y")):
        own_output = own_output + send(part(owned_output, s ^ j, quarter, 0), way).astype(F32)
    own_output = own_output.astype(BF)
    output_pieces = [own_output] + [send(own_output, way) for way in ("x", "y", "d")]
    for way in ("core", "x", "y"):
        small = small + send(small, way)
    over_z, own, small, grad_frames, output_pieces = lax.optimization_barrier(
        (over_z, own, small, grad_frames, output_pieces)
    )

    own = own.astype(F32)
    for piece in over_z:
        own = own + piece.astype(F32)
    own = own.astype(BF)
    kept, theirs = part(own, c, rows, 0), part(own, 1 - c, rows, 0)
    swapped = send(theirs, "core")
    pair = jnp.stack([jnp.where(c == 0, kept, swapped), jnp.where(c == 0, swapped, kept)])
    pieces = [pair] + [send(pair, way) for way in ("x", "y", "d")]
    turn = small + send(small, "z2")
    small = turn + send(turn, "z1")
    grad_pointwise, grad_output = final_call(where, block, pieces, output_pieces)
    return (output[None], grad_frames[None], grad_pointwise, grad_output, small[taps], small[:taps])


def extended_plain(block, sides, width):
    for axis, dim in sides:
        count = lax.axis_size(axis)
        forward = [(i, i + 1) for i in range(count - 1)]
        backward = [(target, source) for source, target in forward]
        low = lax.ppermute(
            lax.slice_in_dim(block, block.shape[dim] - width, None, axis=dim), axis, forward
        )
        high = lax.ppermute(lax.slice_in_dim(block, 0, width, axis=dim), axis, backward)
        block = jnp.concatenate([low, block, high], axis=dim)
    return block


def rounded_term(left, right):
    term = lax.dot_general(
        left, right, (((0,), (0,)), ((), ())), preferred_element_type=jnp.float32
    )
    term = lax.optimization_barrier(term.astype(jnp.bfloat16))
    return term.astype(jnp.float32)


def on_any_mesh(frames, lengths, gain, w_pointwise, w_depthwise, w_output, cotangent):
    frame_count = frames.shape[1]
    width = frames.shape[2]
    taps = w_depthwise.shape[0]
    half_width = (taps - 1) // 2
    full_pointwise, full_output = (
        lax.all_gather(w_pointwise, "fsdp", axis=0, tiled=True),
        lax.all_gather(w_output, "fsdp", axis=0, tiled=True),
    )
    as_float = frames[0].astype(jnp.float32)
    center = jnp.mean(as_float, axis=-1, keepdims=True)
    spread = jnp.mean((as_float - center) ** 2, axis=-1, keepdims=True)
    inverse = lax.rsqrt(spread + EPS)
    normed = (as_float - center) * inverse
    lifted = (normed * gain).astype(jnp.bfloat16)
    position = lax.axis_index("seq") * frame_count + jnp.arange(frame_count, dtype=jnp.int32)
    mask = (position < lengths[0]).astype(jnp.float32)[:, None]
    joined = jnp.dot(lifted, full_pointwise, preferred_element_type=jnp.float32)
    value = joined[:, :width]
    gate_sig = jax.nn.sigmoid(joined[:, width:])
    glu = (value * gate_sig * mask).astype(jnp.bfloat16)
    glu_ext = extended_plain(glu[None], (("seq", 1),), half_width)[0].astype(jnp.float32)
    conv = jnp.zeros((frame_count, width), jnp.float32)
    for offset in range(taps):
        conv = conv + w_depthwise[offset] * glu_ext[offset : offset + frame_count]
    conv_sig = jax.nn.sigmoid(conv)
    swished = (conv * conv_sig).astype(jnp.bfloat16)
    branch = jnp.dot(swished, full_output, preferred_element_type=jnp.float32)
    output = (as_float + branch).astype(jnp.bfloat16)
    branch_grad = (cotangent[0].astype(jnp.float32) * mask).astype(jnp.bfloat16)
    swish_grad = lax.dot_general(
        branch_grad, full_output, (((1,), (1,)), ((), ())), preferred_element_type=jnp.float32
    )
    conv_grad = (swish_grad * conv_sig * (1.0 + conv * (1.0 - conv_sig))).astype(jnp.bfloat16)
    grad_ext = extended_plain(conv_grad[None], (("seq", 1),), half_width)[0].astype(jnp.float32)
    conv_grad_f = conv_grad.astype(jnp.float32)
    glu_grad = jnp.zeros((frame_count, width), jnp.float32)
    tap_rows = []
    for offset in range(taps):
        back = taps - 1 - offset
        glu_grad = glu_grad + w_depthwise[offset] * grad_ext[back : back + frame_count]
        tap_rows.append(jnp.sum(conv_grad_f * glu_ext[offset : offset + frame_count], axis=0))
    glu_grad = glu_grad * mask
    joined_grad = jnp.concatenate(
        [glu_grad * gate_sig, glu_grad * value * gate_sig * (1.0 - gate_sig)], axis=-1
    ).astype(jnp.bfloat16)
    lifted_grad = lax.dot_general(
        joined_grad, full_pointwise, (((1,), (1,)), ((), ())), preferred_element_type=jnp.float32
    )
    gain_term = jnp.sum(lifted_grad * normed, axis=0)
    grad_gain, grad_depthwise = lax.psum((gain_term, jnp.stack(tap_rows, axis=0)), ("seq", "fsdp"))
    scaled = lifted_grad * gain
    norm_grad = inverse * (
        scaled
        - jnp.mean(scaled, axis=-1, keepdims=True)
        - normed * jnp.mean(scaled * normed, axis=-1, keepdims=True)
    )
    grad_frames = (cotangent[0].astype(jnp.float32) + norm_grad).astype(jnp.bfloat16)
    term_pointwise = rounded_term(lifted, joined_grad)
    term_output = rounded_term(swished, branch_grad)
    owned = (
        lax.psum_scatter(
            term_pointwise.astype(jnp.bfloat16), "fsdp", scatter_dimension=0, tiled=True
        ).astype(jnp.float32),
        lax.psum_scatter(
            term_output.astype(jnp.bfloat16), "fsdp", scatter_dimension=0, tiled=True
        ).astype(jnp.float32),
    )
    grad_pointwise, grad_output = (
        lax.psum(owned[0].astype(jnp.bfloat16), "seq").astype(jnp.float32),
        lax.psum(owned[1].astype(jnp.bfloat16), "seq").astype(jnp.float32),
    )
    return (output[None], grad_frames[None], grad_pointwise, grad_output, grad_gain, grad_depthwise)


def solution(mesh):
    in_specs = (
        P("fsdp", "seq", None),
        P("fsdp"),
        P(),
        P("fsdp", None),
        P(),
        P("fsdp", None),
        P("fsdp", "seq", None),
    )
    out_specs = (
        P("fsdp", "seq", None),
        P("fsdp", "seq", None),
        P("fsdp", None),
        P("fsdp", None),
        P(),
        P(),
    )
    known = mesh.shape["seq"] == N_SEQ and mesh.shape["fsdp"] == N_Z * N_CORE
    return jax.shard_map(
        on_slice if known else on_any_mesh,
        mesh=mesh, in_specs=in_specs, out_specs=out_specs, check_vma=False,
    )
```

```python
import functools

import jax
import jax.numpy as jnp
from jax import lax
from jax.experimental import pallas as pl
from jax.experimental.pallas import tpu as pltpu
from jax.sharding import PartitionSpec as P

EPS = 1e-05
BF = jnp.bfloat16
F32 = jnp.float32
BOTH = ("seq", "fsdp")
N_SEQ, N_Z, N_CORE = 4, 4, 2
FAR, NEAR = 32, 16
VMEM_LIMIT = 60 * 1024 * 1024


def device_pairs(move):
    def flat(s, z, c):
        return (s * N_Z + z) * N_CORE + c
    return [
        (flat(s, z, c), flat(*move(s, z, c)))
        for s in range(N_SEQ) for z in range(N_Z) for c in range(N_CORE)
    ]


ACROSS = {
    "core": device_pairs(lambda s, z, c: (s, z, 1 - c)),
    "x": device_pairs(lambda s, z, c: (s ^ 1, z, c)),
    "y": device_pairs(lambda s, z, c: (s ^ 2, z, c)),
    "d": device_pairs(lambda s, z, c: (s ^ 3, z, c)),
    "z1": device_pairs(lambda s, z, c: (s, (z + 1) % N_Z, c)),
    "z2": device_pairs(lambda s, z, c: (s, (z + 2) % N_Z, c)),
    "z3": device_pairs(lambda s, z, c: (s, (z + 3) % N_Z, c)),
}


def send(block, way):
    return lax.ppermute(block, BOTH, ACROSS[way])


def part(block, index, size, axis):
    return lax.dynamic_slice_in_dim(block, index * size, size, axis)


def hint(bytes_accessed=1024):
    return pl.CostEstimate(flops=0, bytes_accessed=bytes_accessed, transcendentals=0)


def joined_kernel(behind, where_ref, lifted_ref, *refs):
    own, came, mine, other = refs[0:2], refs[2:4], refs[4:6], refs[6:8]
    w_value_ref, w_gate_ref, value_ref, sig_ref, glu_ref = refs[-5:]
    z, c, valid = where_ref[1], where_ref[2], where_ref[3]
    rows = own[0].shape[0]
    outs = w_value_ref, w_gate_ref
    for source, pieces, core in ((own, mine, c), (came, other, 1 - c)):
        at = pl.multiple_of((z * N_CORE + core) * rows, 64)
        for side in range(2):
            outs[side][pl.ds(at, rows), :] = source[side][...]
        for index, k in enumerate(behind):
            at = (lax.rem(z + N_Z - k, N_Z) * N_CORE + core) * rows
            for n in range(2):
                low = pl.ds(pl.multiple_of(at + n * (rows // 2), 32), rows // 2)
                for side in range(2):
                    outs[side][low, :] = pieces[n][index, side]
    frames = value_ref.shape[0]
    value = jnp.dot(lifted_ref[...], w_value_ref[...], preferred_element_type=F32)
    value_ref[...] = value[FAR:FAR + frames]
    sig = jax.nn.sigmoid(jnp.dot(lifted_ref[...], w_gate_ref[...], preferred_element_type=F32))
    sig_ref[...] = sig[FAR:FAR + frames]
    position = lax.broadcasted_iota(jnp.int32, sig.shape, 0) - FAR
    glu_ref[...] = jnp.where(position < valid, value * sig, 0.0).astype(BF)


def joined_call(j, behind, where, lifted, w_own, w_came, mine, other, buffers):
    extended, width = lifted.shape
    frames = extended - 2 * FAR
    block = width // N_SEQ
    rows = w_own.shape[0]
    whole = lambda a: pl.BlockSpec(a.shape, lambda i, at: (0,) * a.ndim)
    column = lambda n: pl.BlockSpec((n, block), lambda i, at: (0, at[0] ^ j))
    second = pl.BlockSpec((rows, block), lambda i, at: (0, N_SEQ + (at[0] ^ j)))
    operands = [lifted, w_own, w_own, w_came, w_came, *mine, *other]
    specs = [whole(lifted), column(rows), second, column(rows), second]
    specs += [whole(a) for a in (*mine, *other)]
    aliases = {}
    if buffers:
        aliases = {1 + len(operands) + n: n for n in range(5)}
        operands += buffers
        specs += [pl.BlockSpec(memory_space=pl.ANY)] * 5
    return pl.pallas_call(
        functools.partial(joined_kernel, behind),
        grid_spec=pltpu.PrefetchScalarGridSpec(
            num_scalar_prefetch=1, grid=(1,), in_specs=specs,
            out_specs=[column(width), column(width), column(frames), column(frames), column(extended)],
        ),
        out_shape=[
            jax.ShapeDtypeStruct((width, width), BF), jax.ShapeDtypeStruct((width, width), BF),
            jax.ShapeDtypeStruct((frames, width), F32), jax.ShapeDtypeStruct((frames, width), F32),
            jax.ShapeDtypeStruct((extended, width), BF),
        ],
        input_output_aliases=aliases,
        compiler_params=pltpu.CompilerParams(vmem_limit_bytes=VMEM_LIMIT),
        cost_estimate=hint(),
        name="joined_%d" % j,
    )(where, *operands)


LANES = 128
SUB = 8


def tap_sum(ext_ref, wide, first, height, flip):
    total = None
    for o in range(len(wide)):
        rows = ext_ref[first + o + 1:first + o + 1 + height, :]
        term = rows.reshape(height // SUB, SUB, LANES) * wide[-1 - o if flip else o][None]
        total = term if total is None else total + term
    return total.reshape(height, LANES)


def widened(taps_ref, lanes):
    return [jnp.broadcast_to(taps_ref[k:k + 1, lanes], (SUB, LANES)) for k in range(taps_ref.shape[0])]


def forward_kernel(glu_ref, taps_ref, swished_ref, slope_ref, ext_ref):
    frames, width = swished_ref.shape
    height = 32

    @pl.loop(0, width // LANES)
    def _(b):
        lanes = pl.ds(pl.multiple_of(b * LANES, LANES), LANES)
        wide = widened(taps_ref, lanes)
        ext_ref[...] = glu_ref[:, lanes].astype(F32)
        for first in range(0, frames + 2 * NEAR, height):
            conv = tap_sum(ext_ref, wide, first, height, False)
            sig = jax.nn.sigmoid(conv)
            slope_ref[first:first + height, lanes] = sig * (1.0 + conv * (1.0 - sig))
            low, high = max(first, NEAR), min(first + height, NEAR + frames)
            swished_ref[low - NEAR:high - NEAR, lanes] = (conv * sig)[low - first:high - first].astype(BF)


def forward_call(glu, taps):
    extended, width = glu.shape
    frames = extended - 2 * FAR
    near = frames + 2 * NEAR
    size = width // N_SEQ
    column = lambda rows: pl.BlockSpec((rows, size), lambda i: (0, i))
    return pl.pallas_call(
        forward_kernel,
        grid=(width // size,),
        out_shape=(jax.ShapeDtypeStruct((frames, width), BF), jax.ShapeDtypeStruct((near, width), F32)),
        in_specs=[column(extended), column(taps.shape[0])],
        out_specs=(column(frames), column(near)),
        scratch_shapes=[pltpu.VMEM((extended, LANES), F32)],
        compiler_params=pltpu.CompilerParams(vmem_limit_bytes=VMEM_LIMIT),
        cost_estimate=hint(),
        name="conv_forward",
    )(glu, taps)


def backward_kernel(where_ref, grad_ref, glu_ref, taps_ref, value_ref, sig_ref, *refs):
    mine_ref, send_ref, value_grad_ref, gate_grad_ref, tap_grad_ref, grad_ext_ref, glu_ext_ref, sum_ref = refs[-8:]
    frames, width = value_ref.shape
    taps = taps_ref.shape[0]
    height = 64
    c, valid = where_ref[2], where_ref[3]

    @pl.loop(0, width // LANES)
    def _(b):
        lanes = pl.ds(pl.multiple_of(b * LANES, LANES), LANES)
        wide = widened(taps_ref, lanes)
        grad_ext_ref[...] = grad_ref[:, lanes].astype(F32)
        glu_ext_ref[...] = glu_ref[:, lanes].astype(F32)
        for first in range(0, frames, height):
            at = slice(first, first + height)
            glu_grad = tap_sum(grad_ext_ref, wide, first, height, True)
            position = first + lax.broadcasted_iota(jnp.int32, (height, LANES), 0)
            sig = sig_ref[at, lanes]
            scaled = jnp.where(position < valid, glu_grad, 0.0) * sig
            by_gate = (scaled * value_ref[at, lanes] * (1.0 - sig)).astype(BF)
            scaled = scaled.astype(BF)
            value_grad_ref[at, lanes] = scaled
            gate_grad_ref[at, lanes] = by_gate
            mine_ref[at, lanes] = jnp.where(c == 0, scaled, by_gate)
            send_ref[at, lanes] = jnp.where(c == 0, by_gate, scaled)
        for first in range(0, frames, height):
            grad = grad_ext_ref[first + NEAR:first + NEAR + height, :]
            for k in range(taps):
                low = first + NEAR + k + 1
                term = grad * glu_ext_ref[low:low + height, :]
                total = jnp.sum(term.reshape(height // SUB, SUB, LANES), axis=0)
                sum_ref[k] = total if first == 0 else sum_ref[k] + total
        sum_ref[taps] = jnp.zeros((SUB, LANES), F32)
        tap_grad_ref[:, lanes] = jnp.sum(sum_ref[...], axis=1)


def backward_call(j, where, grad, glu, taps, value, sig, buffers):
    frames, width = value.shape
    size = width // N_SEQ
    count = taps.shape[0]
    column = lambda rows: pl.BlockSpec((rows, size), lambda i, at: (0, at[0] ^ j))
    alone = pl.BlockSpec((frames, size), lambda i, at: (0, 0))
    operands = [grad, glu, taps, value, sig]
    specs = [column(a.shape[0]) for a in operands]
    aliases = {}
    if buffers:
        aliases = {1 + len(operands) + n: 2 + n for n in range(3)}
        operands += buffers
        specs += [pl.BlockSpec(memory_space=pl.ANY)] * 3
    small = jax.ShapeDtypeStruct((frames, size), BF)
    full = jax.ShapeDtypeStruct((frames, width), BF)
    mine, sent, *buffers = pl.pallas_call(
        backward_kernel,
        grid_spec=pltpu.PrefetchScalarGridSpec(
            num_scalar_prefetch=1, grid=(1,), in_specs=specs,
            out_specs=[alone, alone, column(frames), column(frames), column(count + 1)],
            scratch_shapes=[
                pltpu.VMEM((grad.shape[0], LANES), F32), pltpu.VMEM((glu.shape[0], LANES), F32),
                pltpu.VMEM((count + 1, SUB, LANES), F32),
            ],
        ),
        out_shape=[small, small, full, full, jax.ShapeDtypeStruct((count + 1, width), F32)],
        input_output_aliases=aliases,
        compiler_params=pltpu.CompilerParams(vmem_limit_bytes=VMEM_LIMIT),
        cost_estimate=hint(),
        name="conv_backward_%d" % j,
    )(where, *operands)
    return mine, sent, buffers


def edges(frames, cotangent):
    devices = lax.axis_size("seq")
    forward = [(i, i + 1) for i in range(devices - 1)]
    backward = [(target, source) for source, target in forward]
    last, first = jnp.concatenate([frames[-FAR:], cotangent[-NEAR:]]), jnp.concatenate([frames[:FAR], cotangent[:NEAR]])
    return lax.ppermute(last, "seq", forward), lax.ppermute(first, "seq", backward)


def transposed_dot(left, right):
    return lax.dot_general(left, right, (((0,), (0,)), ((), ())), preferred_element_type=F32)


def final_kernel(block, where_ref, *refs):
    pieces, (pointwise_ref, output_ref) = refs[:-2], refs[-2:]
    s = where_ref[0]
    width = N_SEQ * block
    for j in range(N_SEQ):
        for side in range(2):
            at = pl.multiple_of(side * width + (s ^ j) * block, 128)
            pointwise_ref[:, pl.ds(at, block)] = pieces[j][side].astype(F32)
        rows = pieces[N_SEQ + j].shape[0]
        output_ref[pl.ds(pl.multiple_of((s ^ j) * rows, 16), rows), :] = pieces[N_SEQ + j][...].astype(F32)


def final_call(where, block, pointwise_pieces, output_pieces):
    width = N_SEQ * block
    rows = pointwise_pieces[0].shape[1]
    vmem = pl.BlockSpec(memory_space=pltpu.VMEM)
    operands = (*pointwise_pieces, *output_pieces)
    return pl.pallas_call(
        functools.partial(final_kernel, block),
        out_shape=(
            jax.ShapeDtypeStruct((rows, 2 * width), F32),
            jax.ShapeDtypeStruct((rows, width), F32),
        ),
        in_specs=[pl.BlockSpec(memory_space=pltpu.SMEM)] + [vmem] * len(operands),
        out_specs=(vmem, vmem),
        compiler_params=pltpu.CompilerParams(vmem_limit_bytes=VMEM_LIMIT),
        cost_estimate=hint(),
        name="final",
    )(where, *operands)


def after(values, *first):
    return lax.optimization_barrier((values, first))[0]


def on_slice(frames, lengths, gain, w_pointwise, w_depthwise, w_output, cotangent):
    frame_count, width = frames.shape[1:]
    taps = w_depthwise.shape[0]
    block = width // N_SEQ
    rows = width // (N_Z * N_CORE)
    s = lax.axis_index("seq")
    z, c = lax.axis_index("fsdp") // N_CORE, lax.axis_index("fsdp") % N_CORE
    where = jnp.stack([s, z, c, lengths[0] - s * frame_count]).astype(jnp.int32)

    first = jnp.stack([
        lax.dynamic_slice_in_dim(w_pointwise, s * block, block, 1),
        lax.dynamic_slice_in_dim(w_pointwise, width + s * block, block, 1),
    ])
    behind = (1, 3, 2)
    group = [send(first, "z%d" % k) for k in behind]
    w_came = send(w_pointwise, "core")
    low, high = edges(frames[0], cotangent[0])
    frames_low, cotangent_low = low[:FAR], low[FAR:]
    frames_high, cotangent_high = high[:FAR], high[FAR:]

    def norm(x):
        x = x.astype(F32)
        center = jnp.mean(x, axis=-1, keepdims=True)
        inverse = lax.rsqrt(jnp.mean((x - center) ** 2, axis=-1, keepdims=True) + EPS)
        return (x - center) * inverse, inverse

    normed, inverse = norm(frames[0])
    lifted = (normed * gain).astype(BF)
    lifted_edges = (norm(jnp.concatenate([frames_low, frames_high], axis=0))[0] * gain).astype(BF)
    lifted_ext = jnp.concatenate([lifted_edges[:FAR], lifted, lifted_edges[FAR:]], axis=0)
    position = jnp.arange(-NEAR, frame_count + NEAR, dtype=jnp.int32)
    mask = (position < where[3]).astype(F32)[:, None]
    branch_grad = (cotangent[0].astype(F32) * mask[NEAR:-NEAR]).astype(BF)
    branch_ext = jnp.concatenate([
        (cotangent_low.astype(F32) * mask[:NEAR]).astype(BF), branch_grad,
        (cotangent_high.astype(F32) * mask[-NEAR:]).astype(BF),
    ], axis=0)
    halves = [jnp.stack([p[:, h * (rows // 2):(h + 1) * (rows // 2)] for p in group]) for h in range(2)]
    (group_1, group_2), lifted, lifted_ext, branch_grad, branch_ext, w_came = lax.optimization_barrier(
        (halves, lifted, lifted_ext, branch_grad, branch_ext, w_came)
    )

    def joined(j, mine, other, buffers):
        return joined_call(j, behind, where, lifted_ext, w_pointwise, w_came, mine, other, buffers)

    x_1, y_2, x_2, y_1 = send(group_1, "x"), send(group_2, "y"), send(group_2, "x"), send(group_1, "y")
    full_output = lax.all_gather(after(w_output, group_2), "fsdp", axis=0, tiled=True)
    group_1_other, group_2_other = send(group_1, "core"), send(group_2, "core")
    lifted_other = send(lifted, "core")
    turned = lifted.T, lifted_other.T
    buffers = joined(0, [group_1, group_2], [group_1_other, group_2_other], [])
    x_1, y_2, turned, buffers = lax.optimization_barrier((x_1, y_2, turned, buffers))

    d_1, d_2 = send(x_1, "y"), send(y_2, "x")
    x_1_other, y_2_other, x_2_other, y_1_other = (
        send(x_1, "core"), send(y_2, "core"), send(x_2, "core"), send(y_1, "core")
    )
    buffers = joined(1, [x_1, x_2], [x_1_other, x_2_other], buffers)
    buffers = joined(2, [y_1, y_2], [y_1_other, y_2_other], buffers)
    d_1, d_2, buffers = lax.optimization_barrier((d_1, d_2, buffers))
    buffers = joined(3, [d_1, d_2], [send(d_1, "core"), send(d_2, "core")], buffers)
    w_value, w_gate, value, gate_sig, glu = buffers

    swished, slope = forward_call(glu, w_depthwise)
    contract = (((1,), (1,)), ((), ()))
    swish_grad = lax.dot_general(branch_ext, full_output, contract, preferred_element_type=F32)
    conv_grad = (swish_grad * slope).astype(BF)

    def backward(j, buffers):
        mine, sent, buffers = backward_call(j, where, conv_grad, glu, w_depthwise, value, gate_sig, buffers)
        other = send(sent, "core")

        def term(left):
            return jnp.dot(left[0], mine, preferred_element_type=F32) + jnp.dot(
                left[1], other, preferred_element_type=F32
            )

        return term, buffers

    term_3, buffers = backward(3, [])
    term_1, buffers = backward(1, buffers)
    far = term_3(turned).astype(BF)
    from_d = send(far, "d")
    swished = after(swished, far)
    term_output = transposed_dot(swished, branch_grad).astype(BF)
    owned_output = lax.psum_scatter(term_output, "fsdp", scatter_dimension=0, tiled=True)
    term_2, buffers = backward(2, after(buffers, far, term_output))
    near_x = term_1(turned).astype(BF)
    from_x = send(near_x, "x")
    term_0, buffers = backward(0, after(buffers, near_x))
    near_y = term_2(turned).astype(BF)
    from_y = send(near_y, "y")
    last = term_0(turned)
    grad_value, grad_gate, tap_grad = buffers

    grad_value, grad_gate, swished = after((grad_value, grad_gate, swished), near_y)
    lifted_grad = lax.dot_general(
        grad_value, w_value, contract, preferred_element_type=F32
    ) + lax.dot_general(grad_gate, w_gate, contract, preferred_element_type=F32)
    small = jnp.concatenate([tap_grad[:taps], jnp.sum(lifted_grad * normed, axis=0)[None]], axis=0)
    small = small + send(small, "core")
    small = small + send(small, "z2")
    small = small + send(small, "z1")
    branch = jnp.dot(swished, full_output, preferred_element_type=F32)
    output = (frames[0].astype(F32) + branch).astype(BF)
    scaled = lifted_grad * gain
    norm_grad = inverse * (
        scaled
        - jnp.mean(scaled, axis=-1, keepdims=True)
        - normed * jnp.mean(scaled * normed, axis=-1, keepdims=True)
    )
    grad_frames = (cotangent[0].astype(F32) + norm_grad).astype(BF)
    total = (last + from_x.astype(F32) + from_y.astype(F32) + from_d.astype(F32)).astype(BF)
    total, small, grad_frames, output, owned_output = lax.optimization_barrier(
        (total, small, grad_frames, output, owned_output)
    )

    own = part(total, z, 2 * rows, 0)
    over_z = [send(part(total, (z + k) % N_Z, 2 * rows, 0), "z%d" % k) for k in (2, 1, 3)]
    square = (("x", 1), ("y", 2), ("d", 3))
    small_came = [send(small, way) for way, j in square]
    quarter = rows // N_SEQ
    own_output = part(owned_output, s, quarter, 0)
    output_came = [send(part(owned_output, s ^ j, quarter, 0), way) for way, j in square]
    over_z, own, small, small_came, own_output, output_came = lax.optimization_barrier(
        (over_z, own, small, small_came, own_output, output_came)
    )

    own, own_output = own.astype(F32), own_output.astype(F32)
    for piece in over_z:
        own = own + piece.astype(F32)
    for piece in output_came:
        own_output = own_output + piece.astype(F32)
    own, own_output = own.astype(BF), own_output.astype(BF)
    kept, theirs = part(own, c, rows, 0), part(own, 1 - c, rows, 0)
    swapped = send(theirs, "core")
    pair = jnp.stack([jnp.where(c == 0, kept, swapped), jnp.where(c == 0, swapped, kept)])
    pieces = [pair] + [send(pair, way) for way, j in square]
    output_pieces = [own_output] + [send(own_output, way) for way, j in square]
    small = (small + small_came[0]) + (small_came[1] + small_came[2])
    grad_pointwise, grad_output = final_call(where, block, pieces, output_pieces)
    return (output[None], grad_frames[None], grad_pointwise, grad_output, small[taps], small[:taps])


def extended_plain(block, sides, width):
    for axis, dim in sides:
        count = lax.axis_size(axis)
        forward = [(i, i + 1) for i in range(count - 1)]
        backward = [(target, source) for source, target in forward]
        low = lax.ppermute(
            lax.slice_in_dim(block, block.shape[dim] - width, None, axis=dim), axis, forward
        )
        high = lax.ppermute(lax.slice_in_dim(block, 0, width, axis=dim), axis, backward)
        block = jnp.concatenate([low, block, high], axis=dim)
    return block


def rounded_term(left, right):
    term = lax.dot_general(
        left, right, (((0,), (0,)), ((), ())), preferred_element_type=jnp.float32
    )
    term = lax.optimization_barrier(term.astype(jnp.bfloat16))
    return term.astype(jnp.float32)


def on_any_mesh(frames, lengths, gain, w_pointwise, w_depthwise, w_output, cotangent):
    frame_count = frames.shape[1]
    width = frames.shape[2]
    taps = w_depthwise.shape[0]
    half_width = (taps - 1) // 2
    full_pointwise, full_output = (
        lax.all_gather(w_pointwise, "fsdp", axis=0, tiled=True),
        lax.all_gather(w_output, "fsdp", axis=0, tiled=True),
    )
    as_float = frames[0].astype(jnp.float32)
    center = jnp.mean(as_float, axis=-1, keepdims=True)
    spread = jnp.mean((as_float - center) ** 2, axis=-1, keepdims=True)
    inverse = lax.rsqrt(spread + EPS)
    normed = (as_float - center) * inverse
    lifted = (normed * gain).astype(jnp.bfloat16)
    position = lax.axis_index("seq") * frame_count + jnp.arange(frame_count, dtype=jnp.int32)
    mask = (position < lengths[0]).astype(jnp.float32)[:, None]
    joined = jnp.dot(lifted, full_pointwise, preferred_element_type=jnp.float32)
    value = joined[:, :width]
    gate_sig = jax.nn.sigmoid(joined[:, width:])
    glu = (value * gate_sig * mask).astype(jnp.bfloat16)
    glu_ext = extended_plain(glu[None], (("seq", 1),), half_width)[0].astype(jnp.float32)
    conv = jnp.zeros((frame_count, width), jnp.float32)
    for offset in range(taps):
        conv = conv + w_depthwise[offset] * glu_ext[offset : offset + frame_count]
    conv_sig = jax.nn.sigmoid(conv)
    swished = (conv * conv_sig).astype(jnp.bfloat16)
    branch = jnp.dot(swished, full_output, preferred_element_type=jnp.float32)
    output = (as_float + branch).astype(jnp.bfloat16)
    branch_grad = (cotangent[0].astype(jnp.float32) * mask).astype(jnp.bfloat16)
    swish_grad = lax.dot_general(
        branch_grad, full_output, (((1,), (1,)), ((), ())), preferred_element_type=jnp.float32
    )
    conv_grad = (swish_grad * conv_sig * (1.0 + conv * (1.0 - conv_sig))).astype(jnp.bfloat16)
    grad_ext = extended_plain(conv_grad[None], (("seq", 1),), half_width)[0].astype(jnp.float32)
    conv_grad_f = conv_grad.astype(jnp.float32)
    glu_grad = jnp.zeros((frame_count, width), jnp.float32)
    tap_rows = []
    for offset in range(taps):
        back = taps - 1 - offset
        glu_grad = glu_grad + w_depthwise[offset] * grad_ext[back : back + frame_count]
        tap_rows.append(jnp.sum(conv_grad_f * glu_ext[offset : offset + frame_count], axis=0))
    glu_grad = glu_grad * mask
    joined_grad = jnp.concatenate(
        [glu_grad * gate_sig, glu_grad * value * gate_sig * (1.0 - gate_sig)], axis=-1
    ).astype(jnp.bfloat16)
    lifted_grad = lax.dot_general(
        joined_grad, full_pointwise, (((1,), (1,)), ((), ())), preferred_element_type=jnp.float32
    )
    gain_term = jnp.sum(lifted_grad * normed, axis=0)
    grad_gain, grad_depthwise = lax.psum((gain_term, jnp.stack(tap_rows, axis=0)), ("seq", "fsdp"))
    scaled = lifted_grad * gain
    norm_grad = inverse * (
        scaled
        - jnp.mean(scaled, axis=-1, keepdims=True)
        - normed * jnp.mean(scaled * normed, axis=-1, keepdims=True)
    )
    grad_frames = (cotangent[0].astype(jnp.float32) + norm_grad).astype(jnp.bfloat16)
    term_pointwise = rounded_term(lifted, joined_grad)
    term_output = rounded_term(swished, branch_grad)
    owned = (
        lax.psum_scatter(
            term_pointwise.astype(jnp.bfloat16), "fsdp", scatter_dimension=0, tiled=True
        ).astype(jnp.float32),
        lax.psum_scatter(
            term_output.astype(jnp.bfloat16), "fsdp", scatter_dimension=0, tiled=True
        ).astype(jnp.float32),
    )
    grad_pointwise, grad_output = (
        lax.psum(owned[0].astype(jnp.bfloat16), "seq").astype(jnp.float32),
        lax.psum(owned[1].astype(jnp.bfloat16), "seq").astype(jnp.float32),
    )
    return (output[None], grad_frames[None], grad_pointwise, grad_output, grad_gain, grad_depthwise)


def solution(mesh):
    in_specs = (
        P("fsdp", "seq", None),
        P("fsdp"),
        P(),
        P("fsdp", None),
        P(),
        P("fsdp", None),
        P("fsdp", "seq", None),
    )
    out_specs = (
        P("fsdp", "seq", None),
        P("fsdp", "seq", None),
        P("fsdp", None),
        P("fsdp", None),
        P(),
        P(),
    )
    known = mesh.shape["seq"] == N_SEQ and mesh.shape["fsdp"] == N_Z * N_CORE
    return jax.shard_map(
        on_slice if known else on_any_mesh,
        mesh=mesh, in_specs=in_specs, out_specs=out_specs, check_vma=False,
    )
```

```python
import functools

import jax
import jax.numpy as jnp
from jax import lax
from jax.experimental import pallas as pl
from jax.experimental.pallas import tpu as pltpu
from jax.sharding import PartitionSpec as P

EPS = 1e-05
BF = jnp.bfloat16
F32 = jnp.float32
BOTH = ("seq", "fsdp")
N_SEQ, N_Z, N_CORE = 4, 4, 2
FAR, NEAR = 32, 16
VMEM_LIMIT = 60 * 1024 * 1024


def device_pairs(move):
    def flat(s, z, c):
        return (s * N_Z + z) * N_CORE + c
    return [
        (flat(s, z, c), flat(*move(s, z, c)))
        for s in range(N_SEQ) for z in range(N_Z) for c in range(N_CORE)
    ]


ACROSS = {
    "core": device_pairs(lambda s, z, c: (s, z, 1 - c)),
    "x": device_pairs(lambda s, z, c: (s ^ 1, z, c)),
    "y": device_pairs(lambda s, z, c: (s ^ 2, z, c)),
    "d": device_pairs(lambda s, z, c: (s ^ 3, z, c)),
    "z1": device_pairs(lambda s, z, c: (s, (z + 1) % N_Z, c)),
    "z2": device_pairs(lambda s, z, c: (s, (z + 2) % N_Z, c)),
    "z3": device_pairs(lambda s, z, c: (s, (z + 3) % N_Z, c)),
}


def send(block, way):
    return lax.ppermute(block, BOTH, ACROSS[way])


def part(block, index, size, axis):
    return lax.dynamic_slice_in_dim(block, index * size, size, axis)


def hint(bytes_accessed=1024):
    return pl.CostEstimate(flops=0, bytes_accessed=bytes_accessed, transcendentals=0)


def joined_kernel(behind, where_ref, lifted_ref, *refs):
    own, came, mine, other = refs[0:2], refs[2:4], refs[4:6], refs[6:8]
    w_value_ref, w_gate_ref, value_ref, sig_ref, glu_ref = refs[-5:]
    z, c, valid = where_ref[1], where_ref[2], where_ref[3]
    rows = own[0].shape[0]
    outs = w_value_ref, w_gate_ref
    for source, pieces, core in ((own, mine, c), (came, other, 1 - c)):
        at = pl.multiple_of((z * N_CORE + core) * rows, 64)
        for side in range(2):
            outs[side][pl.ds(at, rows), :] = source[side][...]
        for index, k in enumerate(behind):
            at = (lax.rem(z + N_Z - k, N_Z) * N_CORE + core) * rows
            for n in range(2):
                low = pl.ds(pl.multiple_of(at + n * (rows // 2), 32), rows // 2)
                for side in range(2):
                    outs[side][low, :] = pieces[n][index, side]
    frames = value_ref.shape[0]
    value = jnp.dot(lifted_ref[...], w_value_ref[...], preferred_element_type=F32)
    value_ref[...] = value[FAR:FAR + frames]
    sig = jax.nn.sigmoid(jnp.dot(lifted_ref[...], w_gate_ref[...], preferred_element_type=F32))
    sig_ref[...] = sig[FAR:FAR + frames]
    position = lax.broadcasted_iota(jnp.int32, sig.shape, 0) - FAR
    glu_ref[...] = jnp.where(position < valid, value * sig, 0.0).astype(BF)


def joined_call(j, behind, where, lifted, w_own, w_came, mine, other, buffers):
    extended, width = lifted.shape
    frames = extended - 2 * FAR
    block = width // N_SEQ
    rows = w_own.shape[0]
    whole = lambda a: pl.BlockSpec(a.shape, lambda i, at: (0,) * a.ndim)
    column = lambda n: pl.BlockSpec((n, block), lambda i, at: (0, at[0] ^ j))
    second = pl.BlockSpec((rows, block), lambda i, at: (0, N_SEQ + (at[0] ^ j)))
    operands = [lifted, w_own, w_own, w_came, w_came, *mine, *other]
    specs = [whole(lifted), column(rows), second, column(rows), second]
    specs += [whole(a) for a in (*mine, *other)]
    aliases = {}
    if buffers:
        aliases = {1 + len(operands) + n: n for n in range(5)}
        operands += buffers
        specs += [pl.BlockSpec(memory_space=pl.ANY)] * 5
    return pl.pallas_call(
        functools.partial(joined_kernel, behind),
        grid_spec=pltpu.PrefetchScalarGridSpec(
            num_scalar_prefetch=1, grid=(1,), in_specs=specs,
            out_specs=[column(width), column(width), column(frames), column(frames), column(extended)],
        ),
        out_shape=[
            jax.ShapeDtypeStruct((width, width), BF), jax.ShapeDtypeStruct((width, width), BF),
            jax.ShapeDtypeStruct((frames, width), F32), jax.ShapeDtypeStruct((frames, width), F32),
            jax.ShapeDtypeStruct((extended, width), BF),
        ],
        input_output_aliases=aliases,
        compiler_params=pltpu.CompilerParams(vmem_limit_bytes=VMEM_LIMIT),
        cost_estimate=hint(),
        name="joined_%d" % j,
    )(where, *operands)


LANES = 128
SUB = 8


def tap_sum(ext_ref, wide, first, height, flip):
    total = None
    for o in range(len(wide)):
        rows = ext_ref[pl.ds(first + (o + 1), height), :]
        term = rows.reshape(height // SUB, SUB, LANES) * wide[-1 - o if flip else o][None]
        total = term if total is None else total + term
    return total.reshape(height, LANES)


def widened(taps_ref, lanes):
    return [jnp.broadcast_to(taps_ref[k:k + 1, lanes], (SUB, LANES)) for k in range(taps_ref.shape[0])]


def forward_kernel(glu_ref, taps_ref, swished_ref, slope_ref, ext_ref):
    frames, width = swished_ref.shape
    height = 32

    @pl.loop(0, width // LANES)
    def _(b):
        lanes = pl.ds(pl.multiple_of(b * LANES, LANES), LANES)
        wide = widened(taps_ref, lanes)
        ext_ref[...] = glu_ref[:, lanes].astype(F32)
        for first in range(0, frames + 2 * NEAR, height):
            conv = tap_sum(ext_ref, wide, first, height, False)
            sig = jax.nn.sigmoid(conv)
            slope_ref[first:first + height, lanes] = sig * (1.0 + conv * (1.0 - sig))
            low, high = max(first, NEAR), min(first + height, NEAR + frames)
            swished_ref[low - NEAR:high - NEAR, lanes] = (conv * sig)[low - first:high - first].astype(BF)


def forward_call(glu, taps):
    extended, width = glu.shape
    frames = extended - 2 * FAR
    near = frames + 2 * NEAR
    size = width // N_SEQ
    column = lambda rows: pl.BlockSpec((rows, size), lambda i: (0, i))
    return pl.pallas_call(
        forward_kernel,
        grid=(width // size,),
        out_shape=(jax.ShapeDtypeStruct((frames, width), BF), jax.ShapeDtypeStruct((near, width), F32)),
        in_specs=[column(extended), column(taps.shape[0])],
        out_specs=(column(frames), column(near)),
        scratch_shapes=[pltpu.VMEM((extended, LANES), F32)],
        compiler_params=pltpu.CompilerParams(vmem_limit_bytes=VMEM_LIMIT),
        cost_estimate=hint(),
        name="conv_forward",
    )(glu, taps)


def backward_kernel(where_ref, grad_ref, glu_ref, taps_ref, value_ref, sig_ref, *refs):
    mine_ref, send_ref, value_grad_ref, gate_grad_ref, tap_grad_ref, grad_ext_ref, glu_ext_ref, sum_ref = refs[-8:]
    frames, width = value_ref.shape
    taps = taps_ref.shape[0]
    height = 64
    c, valid = where_ref[2], where_ref[3]

    @pl.loop(0, width // LANES)
    def _(b):
        lanes = pl.ds(pl.multiple_of(b * LANES, LANES), LANES)
        wide = widened(taps_ref, lanes)
        grad_ext_ref[...] = grad_ref[:, lanes].astype(F32)
        glu_ext_ref[...] = glu_ref[:, lanes].astype(F32)

        @pl.loop(0, frames // height)
        def _(i):
            first = pl.multiple_of(i * height, height)
            at = pl.ds(first, height)
            glu_grad = tap_sum(grad_ext_ref, wide, first, height, True)
            position = first + lax.broadcasted_iota(jnp.int32, (height, LANES), 0)
            sig = sig_ref[at, lanes]
            scaled = jnp.where(position < valid, glu_grad, 0.0) * sig
            by_gate = (scaled * value_ref[at, lanes] * (1.0 - sig)).astype(BF)
            scaled = scaled.astype(BF)
            value_grad_ref[at, lanes] = scaled
            gate_grad_ref[at, lanes] = by_gate
            mine_ref[at, lanes] = jnp.where(c == 0, scaled, by_gate)
            send_ref[at, lanes] = jnp.where(c == 0, by_gate, scaled)
        sum_ref[...] = jnp.zeros_like(sum_ref)

        @pl.loop(0, frames // height)
        def _(i):
            first = pl.multiple_of(i * height, height)
            grad = grad_ext_ref[pl.ds(pl.multiple_of(first + NEAR, SUB), height), :]
            for k in range(taps):
                term = grad * glu_ext_ref[pl.ds(first + (NEAR + k + 1), height), :]
                sum_ref[k] += jnp.sum(term.reshape(height // SUB, SUB, LANES), axis=0)

        tap_grad_ref[:, lanes] = jnp.sum(sum_ref[...], axis=1)


def backward_call(j, where, grad, glu, taps, value, sig, buffers):
    frames, width = value.shape
    size = width // N_SEQ
    count = taps.shape[0]
    column = lambda rows: pl.BlockSpec((rows, size), lambda i, at: (0, at[0] ^ j))
    alone = pl.BlockSpec((frames, size), lambda i, at: (0, 0))
    operands = [grad, glu, taps, value, sig]
    specs = [column(a.shape[0]) for a in operands]
    aliases = {}
    if buffers:
        aliases = {1 + len(operands) + n: 2 + n for n in range(3)}
        operands += buffers
        specs += [pl.BlockSpec(memory_space=pl.ANY)] * 3
    small = jax.ShapeDtypeStruct((frames, size), BF)
    full = jax.ShapeDtypeStruct((frames, width), BF)
    mine, sent, *buffers = pl.pallas_call(
        backward_kernel,
        grid_spec=pltpu.PrefetchScalarGridSpec(
            num_scalar_prefetch=1, grid=(1,), in_specs=specs,
            out_specs=[alone, alone, column(frames), column(frames), column(count + 1)],
            scratch_shapes=[
                pltpu.VMEM((grad.shape[0], LANES), F32), pltpu.VMEM((glu.shape[0], LANES), F32),
                pltpu.VMEM((count + 1, SUB, LANES), F32),
            ],
        ),
        out_shape=[small, small, full, full, jax.ShapeDtypeStruct((count + 1, width), F32)],
        input_output_aliases=aliases,
        compiler_params=pltpu.CompilerParams(vmem_limit_bytes=VMEM_LIMIT),
        cost_estimate=hint(),
        name="conv_backward_%d" % j,
    )(where, *operands)
    return mine, sent, buffers


def edges(frames, cotangent):
    devices = lax.axis_size("seq")
    forward = [(i, i + 1) for i in range(devices - 1)]
    backward = [(target, source) for source, target in forward]
    last, first = jnp.concatenate([frames[-FAR:], cotangent[-NEAR:]]), jnp.concatenate([frames[:FAR], cotangent[:NEAR]])
    return lax.ppermute(last, "seq", forward), lax.ppermute(first, "seq", backward)


def transposed_dot(left, right):
    return lax.dot_general(left, right, (((0,), (0,)), ((), ())), preferred_element_type=F32)


def final_kernel(block, where_ref, *refs):
    pieces, (pointwise_ref, output_ref) = refs[:-2], refs[-2:]
    s = where_ref[0]
    width = N_SEQ * block
    for j in range(N_SEQ):
        for side in range(2):
            at = pl.multiple_of(side * width + (s ^ j) * block, 128)
            pointwise_ref[:, pl.ds(at, block)] = pieces[j][side].astype(F32)
        rows = pieces[N_SEQ + j].shape[0]
        output_ref[pl.ds(pl.multiple_of((s ^ j) * rows, 16), rows), :] = pieces[N_SEQ + j][...].astype(F32)


def final_call(where, block, pointwise_pieces, output_pieces):
    width = N_SEQ * block
    rows = pointwise_pieces[0].shape[1]
    vmem = pl.BlockSpec(memory_space=pltpu.VMEM)
    operands = (*pointwise_pieces, *output_pieces)
    return pl.pallas_call(
        functools.partial(final_kernel, block),
        out_shape=(
            jax.ShapeDtypeStruct((rows, 2 * width), F32),
            jax.ShapeDtypeStruct((rows, width), F32),
        ),
        in_specs=[pl.BlockSpec(memory_space=pltpu.SMEM)] + [vmem] * len(operands),
        out_specs=(vmem, vmem),
        compiler_params=pltpu.CompilerParams(vmem_limit_bytes=VMEM_LIMIT),
        cost_estimate=hint(),
        name="final",
    )(where, *operands)


def after(values, *first):
    return lax.optimization_barrier((values, first))[0]


def on_slice(frames, lengths, gain, w_pointwise, w_depthwise, w_output, cotangent):
    frame_count, width = frames.shape[1:]
    taps = w_depthwise.shape[0]
    block = width // N_SEQ
    rows = width // (N_Z * N_CORE)
    s = lax.axis_index("seq")
    z, c = lax.axis_index("fsdp") // N_CORE, lax.axis_index("fsdp") % N_CORE
    where = jnp.stack([s, z, c, lengths[0] - s * frame_count]).astype(jnp.int32)

    first = jnp.stack([
        lax.dynamic_slice_in_dim(w_pointwise, s * block, block, 1),
        lax.dynamic_slice_in_dim(w_pointwise, width + s * block, block, 1),
    ])
    behind = (1, 3, 2)
    group = [send(first, "z%d" % k) for k in behind]
    w_came = send(w_pointwise, "core")
    low, high = edges(frames[0], cotangent[0])
    frames_low, cotangent_low = low[:FAR], low[FAR:]
    frames_high, cotangent_high = high[:FAR], high[FAR:]

    def norm(x):
        x = x.astype(F32)
        center = jnp.mean(x, axis=-1, keepdims=True)
        inverse = lax.rsqrt(jnp.mean((x - center) ** 2, axis=-1, keepdims=True) + EPS)
        return (x - center) * inverse, inverse

    normed, inverse = norm(frames[0])
    lifted = (normed * gain).astype(BF)
    lifted_edges = (norm(jnp.concatenate([frames_low, frames_high], axis=0))[0] * gain).astype(BF)
    lifted_ext = jnp.concatenate([lifted_edges[:FAR], lifted, lifted_edges[FAR:]], axis=0)
    position = jnp.arange(-NEAR, frame_count + NEAR, dtype=jnp.int32)
    mask = (position < where[3]).astype(F32)[:, None]
    branch_grad = (cotangent[0].astype(F32) * mask[NEAR:-NEAR]).astype(BF)
    branch_ext = jnp.concatenate([
        (cotangent_low.astype(F32) * mask[:NEAR]).astype(BF), branch_grad,
        (cotangent_high.astype(F32) * mask[-NEAR:]).astype(BF),
    ], axis=0)
    halves = [jnp.stack([p[:, h * (rows // 2):(h + 1) * (rows // 2)] for p in group]) for h in range(2)]
    (group_1, group_2), lifted, lifted_ext, branch_grad, branch_ext, w_came = lax.optimization_barrier(
        (halves, lifted, lifted_ext, branch_grad, branch_ext, w_came)
    )

    def joined(j, mine, other, buffers):
        return joined_call(j, behind, where, lifted_ext, w_pointwise, w_came, mine, other, buffers)

    x_1, y_2, x_2, y_1 = send(group_1, "x"), send(group_2, "y"), send(group_2, "x"), send(group_1, "y")
    full_output = lax.all_gather(after(w_output, group_2), "fsdp", axis=0, tiled=True)
    group_1_other, group_2_other = send(group_1, "core"), send(group_2, "core")
    lifted_other = send(lifted, "core")
    turned = lifted.T, lifted_other.T
    buffers = joined(0, [group_1, group_2], [group_1_other, group_2_other], [])
    x_1, y_2, turned, buffers = lax.optimization_barrier((x_1, y_2, turned, buffers))

    d_1, d_2 = send(x_1, "y"), send(y_2, "x")
    x_1_other, y_2_other, x_2_other, y_1_other = (
        send(x_1, "core"), send(y_2, "core"), send(x_2, "core"), send(y_1, "core")
    )
    buffers = joined(1, [x_1, x_2], [x_1_other, x_2_other], buffers)
    buffers = joined(2, [y_1, y_2], [y_1_other, y_2_other], buffers)
    d_1, d_2, buffers = lax.optimization_barrier((d_1, d_2, buffers))
    buffers = joined(3, [d_1, d_2], [send(d_1, "core"), send(d_2, "core")], buffers)
    w_value, w_gate, value, gate_sig, glu = buffers

    swished, slope = forward_call(glu, w_depthwise)
    contract = (((1,), (1,)), ((), ()))
    swish_grad = lax.dot_general(branch_ext, full_output, contract, preferred_element_type=F32)
    conv_grad = (swish_grad * slope).astype(BF)

    def backward(j, buffers):
        mine, sent, buffers = backward_call(j, where, conv_grad, glu, w_depthwise, value, gate_sig, buffers)
        other = send(sent, "core")

        def term(left):
            return jnp.dot(left[0], mine, preferred_element_type=F32) + jnp.dot(
                left[1], other, preferred_element_type=F32
            )

        return term, buffers

    term_3, buffers = backward(3, [])
    term_1, buffers = backward(1, buffers)
    far = term_3(turned).astype(BF)
    from_d = send(far, "d")
    swished = after(swished, far)
    term_output = transposed_dot(swished, branch_grad).astype(BF)
    owned_output = lax.psum_scatter(term_output, "fsdp", scatter_dimension=0, tiled=True)
    term_2, buffers = backward(2, after(buffers, far, term_output))
    near_x = term_1(turned).astype(BF)
    from_x = send(near_x, "x")
    term_0, buffers = backward(0, after(buffers, near_x))
    near_y = term_2(turned).astype(BF)
    from_y = send(near_y, "y")
    last = term_0(turned)
    grad_value, grad_gate, tap_grad = buffers

    grad_value, grad_gate, swished = after((grad_value, grad_gate, swished), near_y)
    lifted_grad = lax.dot_general(
        grad_value, w_value, contract, preferred_element_type=F32
    ) + lax.dot_general(grad_gate, w_gate, contract, preferred_element_type=F32)
    small = jnp.concatenate([tap_grad[:taps], jnp.sum(lifted_grad * normed, axis=0)[None]], axis=0)
    small = small + send(small, "core")
    branch = jnp.dot(swished, full_output, preferred_element_type=F32)
    output = (frames[0].astype(F32) + branch).astype(BF)
    scaled = lifted_grad * gain
    norm_grad = inverse * (
        scaled
        - jnp.mean(scaled, axis=-1, keepdims=True)
        - normed * jnp.mean(scaled * normed, axis=-1, keepdims=True)
    )
    grad_frames = (cotangent[0].astype(F32) + norm_grad).astype(BF)
    total = (last + from_x.astype(F32) + from_y.astype(F32) + from_d.astype(F32)).astype(BF)
    total, small, grad_frames, output, owned_output = lax.optimization_barrier(
        (total, small, grad_frames, output, owned_output)
    )

    own = part(total, z, 2 * rows, 0)
    over_z = [send(part(total, (z + k) % N_Z, 2 * rows, 0), "z%d" % k) for k in (2, 1, 3)]
    square = (("x", 1), ("y", 2), ("d", 3))
    small_came = [send(small, way) for way, j in square]
    quarter = rows // N_SEQ
    own_output = part(owned_output, s, quarter, 0)
    output_came = [send(part(owned_output, s ^ j, quarter, 0), way) for way, j in square]
    over_z, own, small, small_came, own_output, output_came = lax.optimization_barrier(
        (over_z, own, small, small_came, own_output, output_came)
    )

    own, own_output = own.astype(F32), own_output.astype(F32)
    for piece in over_z:
        own = own + piece.astype(F32)
    for piece in output_came:
        own_output = own_output + piece.astype(F32)
    own, own_output = own.astype(BF), own_output.astype(BF)
    kept, theirs = part(own, c, rows, 0), part(own, 1 - c, rows, 0)
    swapped = send(theirs, "core")
    pair = jnp.stack([jnp.where(c == 0, kept, swapped), jnp.where(c == 0, swapped, kept)])
    small = (small + small_came[0]) + (small_came[1] + small_came[2])
    pair, small = lax.optimization_barrier((pair, small))
    pieces = [pair] + [send(pair, way) for way, j in square]
    small = small + send(small, "z2")
    small = small + send(small, "z1")
    output_pieces = [own_output] + [send(own_output, way) for way, j in square]
    grad_pointwise, grad_output = final_call(where, block, pieces, output_pieces)
    return (output[None], grad_frames[None], grad_pointwise, grad_output, small[taps], small[:taps])


def extended_plain(block, sides, width):
    for axis, dim in sides:
        count = lax.axis_size(axis)
        forward = [(i, i + 1) for i in range(count - 1)]
        backward = [(target, source) for source, target in forward]
        low = lax.ppermute(
            lax.slice_in_dim(block, block.shape[dim] - width, None, axis=dim), axis, forward
        )
        high = lax.ppermute(lax.slice_in_dim(block, 0, width, axis=dim), axis, backward)
        block = jnp.concatenate([low, block, high], axis=dim)
    return block


def rounded_term(left, right):
    term = lax.dot_general(
        left, right, (((0,), (0,)), ((), ())), preferred_element_type=jnp.float32
    )
    term = lax.optimization_barrier(term.astype(jnp.bfloat16))
    return term.astype(jnp.float32)


def on_any_mesh(frames, lengths, gain, w_pointwise, w_depthwise, w_output, cotangent):
    frame_count = frames.shape[1]
    width = frames.shape[2]
    taps = w_depthwise.shape[0]
    half_width = (taps - 1) // 2
    full_pointwise, full_output = (
        lax.all_gather(w_pointwise, "fsdp", axis=0, tiled=True),
        lax.all_gather(w_output, "fsdp", axis=0, tiled=True),
    )
    as_float = frames[0].astype(jnp.float32)
    center = jnp.mean(as_float, axis=-1, keepdims=True)
    spread = jnp.mean((as_float - center) ** 2, axis=-1, keepdims=True)
    inverse = lax.rsqrt(spread + EPS)
    normed = (as_float - center) * inverse
    lifted = (normed * gain).astype(jnp.bfloat16)
    position = lax.axis_index("seq") * frame_count + jnp.arange(frame_count, dtype=jnp.int32)
    mask = (position < lengths[0]).astype(jnp.float32)[:, None]
    joined = jnp.dot(lifted, full_pointwise, preferred_element_type=jnp.float32)
    value = joined[:, :width]
    gate_sig = jax.nn.sigmoid(joined[:, width:])
    glu = (value * gate_sig * mask).astype(jnp.bfloat16)
    glu_ext = extended_plain(glu[None], (("seq", 1),), half_width)[0].astype(jnp.float32)
    conv = jnp.zeros((frame_count, width), jnp.float32)
    for offset in range(taps):
        conv = conv + w_depthwise[offset] * glu_ext[offset : offset + frame_count]
    conv_sig = jax.nn.sigmoid(conv)
    swished = (conv * conv_sig).astype(jnp.bfloat16)
    branch = jnp.dot(swished, full_output, preferred_element_type=jnp.float32)
    output = (as_float + branch).astype(jnp.bfloat16)
    branch_grad = (cotangent[0].astype(jnp.float32) * mask).astype(jnp.bfloat16)
    swish_grad = lax.dot_general(
        branch_grad, full_output, (((1,), (1,)), ((), ())), preferred_element_type=jnp.float32
    )
    conv_grad = (swish_grad * conv_sig * (1.0 + conv * (1.0 - conv_sig))).astype(jnp.bfloat16)
    grad_ext = extended_plain(conv_grad[None], (("seq", 1),), half_width)[0].astype(jnp.float32)
    conv_grad_f = conv_grad.astype(jnp.float32)
    glu_grad = jnp.zeros((frame_count, width), jnp.float32)
    tap_rows = []
    for offset in range(taps):
        back = taps - 1 - offset
        glu_grad = glu_grad + w_depthwise[offset] * grad_ext[back : back + frame_count]
        tap_rows.append(jnp.sum(conv_grad_f * glu_ext[offset : offset + frame_count], axis=0))
    glu_grad = glu_grad * mask
    joined_grad = jnp.concatenate(
        [glu_grad * gate_sig, glu_grad * value * gate_sig * (1.0 - gate_sig)], axis=-1
    ).astype(jnp.bfloat16)
    lifted_grad = lax.dot_general(
        joined_grad, full_pointwise, (((1,), (1,)), ((), ())), preferred_element_type=jnp.float32
    )
    gain_term = jnp.sum(lifted_grad * normed, axis=0)
    grad_gain, grad_depthwise = lax.psum((gain_term, jnp.stack(tap_rows, axis=0)), ("seq", "fsdp"))
    scaled = lifted_grad * gain
    norm_grad = inverse * (
        scaled
        - jnp.mean(scaled, axis=-1, keepdims=True)
        - normed * jnp.mean(scaled * normed, axis=-1, keepdims=True)
    )
    grad_frames = (cotangent[0].astype(jnp.float32) + norm_grad).astype(jnp.bfloat16)
    term_pointwise = rounded_term(lifted, joined_grad)
    term_output = rounded_term(swished, branch_grad)
    owned = (
        lax.psum_scatter(
            term_pointwise.astype(jnp.bfloat16), "fsdp", scatter_dimension=0, tiled=True
        ).astype(jnp.float32),
        lax.psum_scatter(
            term_output.astype(jnp.bfloat16), "fsdp", scatter_dimension=0, tiled=True
        ).astype(jnp.float32),
    )
    grad_pointwise, grad_output = (
        lax.psum(owned[0].astype(jnp.bfloat16), "seq").astype(jnp.float32),
        lax.psum(owned[1].astype(jnp.bfloat16), "seq").astype(jnp.float32),
    )
    return (output[None], grad_frames[None], grad_pointwise, grad_output, grad_gain, grad_depthwise)


def solution(mesh):
    in_specs = (
        P("fsdp", "seq", None),
        P("fsdp"),
        P(),
        P("fsdp", None),
        P(),
        P("fsdp", None),
        P("fsdp", "seq", None),
    )
    out_specs = (
        P("fsdp", "seq", None),
        P("fsdp", "seq", None),
        P("fsdp", None),
        P("fsdp", None),
        P(),
        P(),
    )
    known = mesh.shape["seq"] == N_SEQ and mesh.shape["fsdp"] == N_Z * N_CORE
    return jax.shard_map(
        on_slice if known else on_any_mesh,
        mesh=mesh, in_specs=in_specs, out_specs=out_specs, check_vma=False,
    )
```

```python
import functools

import jax
import jax.numpy as jnp
from jax import lax
from jax.experimental import pallas as pl
from jax.experimental.pallas import tpu as pltpu
from jax.sharding import PartitionSpec as P

EPS = 1e-05
BF = jnp.bfloat16
F32 = jnp.float32
BOTH = ("seq", "fsdp")
N_SEQ, N_Z, N_CORE = 4, 4, 2
FAR, NEAR = 32, 16
VMEM_LIMIT = 60 * 1024 * 1024


def device_pairs(move):
    def flat(s, z, c):
        return (s * N_Z + z) * N_CORE + c
    return [
        (flat(s, z, c), flat(*move(s, z, c)))
        for s in range(N_SEQ) for z in range(N_Z) for c in range(N_CORE)
    ]


ACROSS = {
    "core": device_pairs(lambda s, z, c: (s, z, 1 - c)),
    "x": device_pairs(lambda s, z, c: (s ^ 1, z, c)),
    "y": device_pairs(lambda s, z, c: (s ^ 2, z, c)),
    "d": device_pairs(lambda s, z, c: (s ^ 3, z, c)),
    "z1": device_pairs(lambda s, z, c: (s, (z + 1) % N_Z, c)),
    "z2": device_pairs(lambda s, z, c: (s, (z + 2) % N_Z, c)),
    "z3": device_pairs(lambda s, z, c: (s, (z + 3) % N_Z, c)),
}


def send(block, way):
    return lax.ppermute(block, BOTH, ACROSS[way])


def part(block, index, size, axis):
    return lax.dynamic_slice_in_dim(block, index * size, size, axis)


def hint(bytes_accessed=1024):
    return pl.CostEstimate(flops=0, bytes_accessed=bytes_accessed, transcendentals=0)


def joined_kernel(behind, where_ref, lifted_ref, *refs):
    own, came, mine, other = refs[0:2], refs[2:4], refs[4:6], refs[6:8]
    w_value_ref, w_gate_ref, value_ref, sig_ref, glu_ref = refs[-5:]
    z, c, valid = where_ref[1], where_ref[2], where_ref[3]
    rows = own[0].shape[0]
    outs = w_value_ref, w_gate_ref
    for source, pieces, core in ((own, mine, c), (came, other, 1 - c)):
        at = pl.multiple_of((z * N_CORE + core) * rows, 64)
        for side in range(2):
            outs[side][pl.ds(at, rows), :] = source[side][...]
        for index, k in enumerate(behind):
            at = (lax.rem(z + N_Z - k, N_Z) * N_CORE + core) * rows
            for n in range(2):
                low = pl.ds(pl.multiple_of(at + n * (rows // 2), 32), rows // 2)
                for side in range(2):
                    outs[side][low, :] = pieces[n][index, side]
    frames = value_ref.shape[0]
    value = jnp.dot(lifted_ref[...], w_value_ref[...], preferred_element_type=F32)
    value_ref[...] = value[FAR:FAR + frames]
    sig = jax.nn.sigmoid(jnp.dot(lifted_ref[...], w_gate_ref[...], preferred_element_type=F32))
    sig_ref[...] = sig[FAR:FAR + frames]
    position = lax.broadcasted_iota(jnp.int32, sig.shape, 0) - FAR
    glu_ref[...] = jnp.where(position < valid, value * sig, 0.0).astype(BF)


def joined_call(j, behind, where, lifted, w_own, w_came, mine, other, buffers):
    extended, width = lifted.shape
    frames = extended - 2 * FAR
    block = width // N_SEQ
    rows = w_own.shape[0]
    whole = lambda a: pl.BlockSpec(a.shape, lambda i, at: (0,) * a.ndim)
    column = lambda n: pl.BlockSpec((n, block), lambda i, at: (0, at[0] ^ j))
    second = pl.BlockSpec((rows, block), lambda i, at: (0, N_SEQ + (at[0] ^ j)))
    operands = [lifted, w_own, w_own, w_came, w_came, *mine, *other]
    specs = [whole(lifted), column(rows), second, column(rows), second]
    specs += [whole(a) for a in (*mine, *other)]
    aliases = {}
    if buffers:
        aliases = {1 + len(operands) + n: n for n in range(5)}
        operands += buffers
        specs += [pl.BlockSpec(memory_space=pl.ANY)] * 5
    return pl.pallas_call(
        functools.partial(joined_kernel, behind),
        grid_spec=pltpu.PrefetchScalarGridSpec(
            num_scalar_prefetch=1, grid=(1,), in_specs=specs,
            out_specs=[column(width), column(width), column(frames), column(frames), column(extended)],
        ),
        out_shape=[
            jax.ShapeDtypeStruct((width, width), BF), jax.ShapeDtypeStruct((width, width), BF),
            jax.ShapeDtypeStruct((frames, width), F32), jax.ShapeDtypeStruct((frames, width), F32),
            jax.ShapeDtypeStruct((extended, width), BF),
        ],
        input_output_aliases=aliases,
        compiler_params=pltpu.CompilerParams(vmem_limit_bytes=VMEM_LIMIT),
        cost_estimate=hint(),
        name="joined_%d" % j,
    )(where, *operands)


LANES = 128
SUB = 8


def tap_sum(ext_ref, wide, first, height, flip):
    total = None
    for o in range(len(wide)):
        rows = ext_ref[pl.ds(first + (o + 1), height), :]
        term = rows.reshape(height // SUB, SUB, LANES) * wide[-1 - o if flip else o][None]
        total = term if total is None else total + term
    return total.reshape(height, LANES)


def widened(taps_ref, lanes):
    return [jnp.broadcast_to(taps_ref[k:k + 1, lanes], (SUB, LANES)) for k in range(taps_ref.shape[0])]


def forward_kernel(glu_ref, taps_ref, swished_ref, slope_ref, ext_ref):
    frames, width = swished_ref.shape
    height = 32

    @pl.loop(0, width // LANES)
    def _(b):
        lanes = pl.ds(pl.multiple_of(b * LANES, LANES), LANES)
        wide = widened(taps_ref, lanes)
        ext_ref[...] = glu_ref[:, lanes].astype(F32)
        for first in range(0, frames + 2 * NEAR, height):
            conv = tap_sum(ext_ref, wide, first, height, False)
            sig = jax.nn.sigmoid(conv)
            slope_ref[first:first + height, lanes] = sig * (1.0 + conv * (1.0 - sig))
            low, high = max(first, NEAR), min(first + height, NEAR + frames)
            swished_ref[low - NEAR:high - NEAR, lanes] = (conv * sig)[low - first:high - first].astype(BF)


def forward_call(glu, taps):
    extended, width = glu.shape
    frames = extended - 2 * FAR
    near = frames + 2 * NEAR
    size = width // N_SEQ
    column = lambda rows: pl.BlockSpec((rows, size), lambda i: (0, i))
    return pl.pallas_call(
        forward_kernel,
        grid=(width // size,),
        out_shape=(jax.ShapeDtypeStruct((frames, width), BF), jax.ShapeDtypeStruct((near, width), F32)),
        in_specs=[column(extended), column(taps.shape[0])],
        out_specs=(column(frames), column(near)),
        scratch_shapes=[pltpu.VMEM((extended, LANES), F32)],
        compiler_params=pltpu.CompilerParams(vmem_limit_bytes=VMEM_LIMIT),
        cost_estimate=hint(),
        name="conv_forward",
    )(glu, taps)


def backward_kernel(where_ref, grad_ref, glu_ref, taps_ref, value_ref, sig_ref, *refs):
    mine_ref, send_ref, value_grad_ref, gate_grad_ref, tap_grad_ref, grad_ext_ref, glu_ext_ref, sum_ref = refs[-8:]
    frames, width = value_ref.shape
    taps = taps_ref.shape[0]
    height = 64
    c, valid = where_ref[2], where_ref[3]

    @pl.loop(0, width // LANES)
    def _(b):
        lanes = pl.ds(pl.multiple_of(b * LANES, LANES), LANES)
        wide = widened(taps_ref, lanes)
        grad_ext_ref[...] = grad_ref[:, lanes].astype(F32)
        glu_ext_ref[...] = glu_ref[:, lanes].astype(F32)

        @pl.loop(0, frames // height)
        def _(i):
            first = pl.multiple_of(i * height, height)
            at = pl.ds(first, height)
            glu_grad = tap_sum(grad_ext_ref, wide, first, height, True)
            position = first + lax.broadcasted_iota(jnp.int32, (height, LANES), 0)
            sig = sig_ref[at, lanes]
            scaled = jnp.where(position < valid, glu_grad, 0.0) * sig
            by_gate = (scaled * value_ref[at, lanes] * (1.0 - sig)).astype(BF)
            scaled = scaled.astype(BF)
            value_grad_ref[at, lanes] = scaled
            gate_grad_ref[at, lanes] = by_gate
            mine_ref[at, lanes] = jnp.where(c == 0, scaled, by_gate)
            send_ref[at, lanes] = jnp.where(c == 0, by_gate, scaled)
        sum_ref[...] = jnp.zeros_like(sum_ref)

        @pl.loop(0, frames // height)
        def _(i):
            first = pl.multiple_of(i * height, height)
            grad = grad_ext_ref[pl.ds(pl.multiple_of(first + NEAR, SUB), height), :]
            for k in range(taps):
                term = grad * glu_ext_ref[pl.ds(first + (NEAR + k + 1), height), :]
                sum_ref[k] += jnp.sum(term.reshape(height // SUB, SUB, LANES), axis=0)

        tap_grad_ref[:, lanes] = jnp.sum(sum_ref[...], axis=1)


def backward_call(j, where, grad, glu, taps, value, sig, buffers):
    frames, width = value.shape
    size = width // N_SEQ
    count = taps.shape[0]
    column = lambda rows: pl.BlockSpec((rows, size), lambda i, at: (0, at[0] ^ j))
    alone = pl.BlockSpec((frames, size), lambda i, at: (0, 0))
    operands = [grad, glu, taps, value, sig]
    specs = [column(a.shape[0]) for a in operands]
    aliases = {}
    if buffers:
        aliases = {1 + len(operands) + n: 2 + n for n in range(3)}
        operands += buffers
        specs += [pl.BlockSpec(memory_space=pl.ANY)] * 3
    small = jax.ShapeDtypeStruct((frames, size), BF)
    full = jax.ShapeDtypeStruct((frames, width), BF)
    mine, sent, *buffers = pl.pallas_call(
        backward_kernel,
        grid_spec=pltpu.PrefetchScalarGridSpec(
            num_scalar_prefetch=1, grid=(1,), in_specs=specs,
            out_specs=[alone, alone, column(frames), column(frames), column(count + 1)],
            scratch_shapes=[
                pltpu.VMEM((grad.shape[0], LANES), F32), pltpu.VMEM((glu.shape[0], LANES), F32),
                pltpu.VMEM((count + 1, SUB, LANES), F32),
            ],
        ),
        out_shape=[small, small, full, full, jax.ShapeDtypeStruct((count + 1, width), F32)],
        input_output_aliases=aliases,
        compiler_params=pltpu.CompilerParams(vmem_limit_bytes=VMEM_LIMIT),
        cost_estimate=hint(),
        name="conv_backward_%d" % j,
    )(where, *operands)
    return mine, sent, buffers


def edges(frames, cotangent):
    devices = lax.axis_size("seq")
    forward = [(i, i + 1) for i in range(devices - 1)]
    backward = [(target, source) for source, target in forward]
    last, first = jnp.concatenate([frames[-FAR:], cotangent[-NEAR:]]), jnp.concatenate([frames[:FAR], cotangent[:NEAR]])
    return lax.ppermute(last, "seq", forward), lax.ppermute(first, "seq", backward)


def transposed_dot(left, right):
    return lax.dot_general(left, right, (((0,), (0,)), ((), ())), preferred_element_type=F32)


def final_kernel(block, where_ref, *refs):
    pieces, (pointwise_ref, output_ref) = refs[:-2], refs[-2:]
    s = where_ref[0]
    width = N_SEQ * block
    for j in range(N_SEQ):
        for side in range(2):
            at = pl.multiple_of(side * width + (s ^ j) * block, 128)
            pointwise_ref[:, pl.ds(at, block)] = pieces[j][side].astype(F32)
        rows = pieces[N_SEQ + j].shape[0]
        output_ref[pl.ds(pl.multiple_of((s ^ j) * rows, 16), rows), :] = pieces[N_SEQ + j][...].astype(F32)


def final_call(where, block, pointwise_pieces, output_pieces):
    width = N_SEQ * block
    rows = pointwise_pieces[0].shape[1]
    vmem = pl.BlockSpec(memory_space=pltpu.VMEM)
    operands = (*pointwise_pieces, *output_pieces)
    return pl.pallas_call(
        functools.partial(final_kernel, block),
        out_shape=(
            jax.ShapeDtypeStruct((rows, 2 * width), F32),
            jax.ShapeDtypeStruct((rows, width), F32),
        ),
        in_specs=[pl.BlockSpec(memory_space=pltpu.SMEM)] + [vmem] * len(operands),
        out_specs=(vmem, vmem),
        compiler_params=pltpu.CompilerParams(vmem_limit_bytes=VMEM_LIMIT),
        cost_estimate=hint(),
        name="final",
    )(where, *operands)


def after(values, *first):
    return lax.optimization_barrier((values, first))[0]


def on_slice(frames, lengths, gain, w_pointwise, w_depthwise, w_output, cotangent):
    frame_count, width = frames.shape[1:]
    taps = w_depthwise.shape[0]
    block = width // N_SEQ
    rows = width // (N_Z * N_CORE)
    s = lax.axis_index("seq")
    z, c = lax.axis_index("fsdp") // N_CORE, lax.axis_index("fsdp") % N_CORE
    where = jnp.stack([s, z, c, lengths[0] - s * frame_count]).astype(jnp.int32)

    first = jnp.stack([
        lax.dynamic_slice_in_dim(w_pointwise, s * block, block, 1),
        lax.dynamic_slice_in_dim(w_pointwise, width + s * block, block, 1),
    ])
    behind = (1, 3, 2)
    group = [send(first, "z%d" % k) for k in behind]
    w_came = send(w_pointwise, "core")
    low, high = edges(frames[0], cotangent[0])
    frames_low, cotangent_low = low[:FAR], low[FAR:]
    frames_high, cotangent_high = high[:FAR], high[FAR:]

    def norm(x):
        x = x.astype(F32)
        center = jnp.mean(x, axis=-1, keepdims=True)
        inverse = lax.rsqrt(jnp.mean((x - center) ** 2, axis=-1, keepdims=True) + EPS)
        return (x - center) * inverse, inverse

    normed, inverse = norm(frames[0])
    lifted = (normed * gain).astype(BF)
    lifted_edges = (norm(jnp.concatenate([frames_low, frames_high], axis=0))[0] * gain).astype(BF)
    lifted_ext = jnp.concatenate([lifted_edges[:FAR], lifted, lifted_edges[FAR:]], axis=0)
    position = jnp.arange(-NEAR, frame_count + NEAR, dtype=jnp.int32)
    mask = (position < where[3]).astype(F32)[:, None]
    branch_grad = (cotangent[0].astype(F32) * mask[NEAR:-NEAR]).astype(BF)
    branch_ext = jnp.concatenate([
        (cotangent_low.astype(F32) * mask[:NEAR]).astype(BF), branch_grad,
        (cotangent_high.astype(F32) * mask[-NEAR:]).astype(BF),
    ], axis=0)
    halves = [jnp.stack([p[:, h * (rows // 2):(h + 1) * (rows // 2)] for p in group]) for h in range(2)]
    (group_1, group_2), lifted, lifted_ext, branch_grad, branch_ext, w_came = lax.optimization_barrier(
        (halves, lifted, lifted_ext, branch_grad, branch_ext, w_came)
    )

    def joined(j, mine, other, buffers):
        return joined_call(j, behind, where, lifted_ext, w_pointwise, w_came, mine, other, buffers)

    x_1, y_2, x_2, y_1 = send(group_1, "x"), send(group_2, "y"), send(group_2, "x"), send(group_1, "y")
    full_output = lax.all_gather(after(w_output, group_2), "fsdp", axis=0, tiled=True)
    group_1_other, group_2_other = send(group_1, "core"), send(group_2, "core")
    lifted_other = send(lifted, "core")
    turned = lifted.T, lifted_other.T
    buffers = joined(0, [group_1, group_2], [group_1_other, group_2_other], [])
    turned, buffers = lax.optimization_barrier((turned, buffers))
    x_1, y_2, x_2, y_1, buffers = lax.optimization_barrier((x_1, y_2, x_2, y_1, buffers))

    d_1, d_2 = send(x_1, "y"), send(y_2, "x")
    x_1_other, y_2_other, x_2_other, y_1_other = (
        send(x_1, "core"), send(y_2, "core"), send(x_2, "core"), send(y_1, "core")
    )
    buffers = joined(1, [x_1, x_2], [x_1_other, x_2_other], buffers)
    buffers = joined(2, [y_1, y_2], [y_1_other, y_2_other], buffers)
    d_1, d_2, buffers = lax.optimization_barrier((d_1, d_2, buffers))
    buffers = joined(3, [d_1, d_2], [send(d_1, "core"), send(d_2, "core")], buffers)
    w_value, w_gate, value, gate_sig, glu = buffers

    swished, slope = forward_call(glu, w_depthwise)
    contract = (((1,), (1,)), ((), ()))
    swish_grad = lax.dot_general(branch_ext, full_output, contract, preferred_element_type=F32)
    conv_grad = (swish_grad * slope).astype(BF)

    def backward(j, buffers):
        mine, sent, buffers = backward_call(j, where, conv_grad, glu, w_depthwise, value, gate_sig, buffers)
        other = send(sent, "core")

        def term(left):
            return jnp.dot(left[0], mine, preferred_element_type=F32) + jnp.dot(
                left[1], other, preferred_element_type=F32
            )

        return term, buffers

    term_3, buffers = backward(3, [])
    term_1, buffers = backward(1, buffers)
    far = term_3(turned).astype(BF)
    from_d = send(far, "d")
    swished = after(swished, far)
    term_output = transposed_dot(swished, branch_grad).astype(BF)
    owned_output = lax.psum_scatter(term_output, "fsdp", scatter_dimension=0, tiled=True)
    term_2, buffers = backward(2, after(buffers, far, term_output))
    near_x = term_1(turned).astype(BF)
    from_x = send(near_x, "x")
    term_0, buffers = backward(0, after(buffers, near_x))
    near_y = term_2(turned).astype(BF)
    from_y = send(near_y, "y")
    last = term_0(turned)
    grad_value, grad_gate, tap_grad = buffers

    grad_value, grad_gate, swished = after((grad_value, grad_gate, swished), near_y)
    lifted_grad = lax.dot_general(
        grad_value, w_value, contract, preferred_element_type=F32
    ) + lax.dot_general(grad_gate, w_gate, contract, preferred_element_type=F32)
    small = jnp.concatenate([tap_grad[:taps], jnp.sum(lifted_grad * normed, axis=0)[None]], axis=0)
    small = small + send(small, "core")
    branch = jnp.dot(swished, full_output, preferred_element_type=F32)
    output = (frames[0].astype(F32) + branch).astype(BF)
    scaled = lifted_grad * gain
    norm_grad = inverse * (
        scaled
        - jnp.mean(scaled, axis=-1, keepdims=True)
        - normed * jnp.mean(scaled * normed, axis=-1, keepdims=True)
    )
    grad_frames = (cotangent[0].astype(F32) + norm_grad).astype(BF)
    total = (last + from_x.astype(F32) + from_y.astype(F32) + from_d.astype(F32)).astype(BF)
    total, small, grad_frames, output, owned_output = lax.optimization_barrier(
        (total, small, grad_frames, output, owned_output)
    )

    own = part(total, z, 2 * rows, 0)
    over_z = [send(part(total, (z + k) % N_Z, 2 * rows, 0), "z%d" % k) for k in (2, 1, 3)]
    square = (("x", 1), ("y", 2), ("d", 3))
    small_came = [send(small, way) for way, j in square]
    quarter = rows // N_SEQ
    own_output = part(owned_output, s, quarter, 0)
    output_came = [send(part(owned_output, s ^ j, quarter, 0), way) for way, j in square]
    over_z, own, small, small_came, own_output, output_came = lax.optimization_barrier(
        (over_z, own, small, small_came, own_output, output_came)
    )

    own, own_output = own.astype(F32), own_output.astype(F32)
    for piece in over_z:
        own = own + piece.astype(F32)
    for piece in output_came:
        own_output = own_output + piece.astype(F32)
    own, own_output = own.astype(BF), own_output.astype(BF)
    kept, theirs = part(own, c, rows, 0), part(own, 1 - c, rows, 0)
    swapped = send(theirs, "core")
    pair = jnp.stack([jnp.where(c == 0, kept, swapped), jnp.where(c == 0, swapped, kept)])
    small = (small + small_came[0]) + (small_came[1] + small_came[2])
    pair, small = lax.optimization_barrier((pair, small))
    pieces = [pair] + [send(pair, way) for way, j in square]
    small = small + send(small, "z2")
    small = small + send(small, "z1")
    output_pieces = [own_output] + [send(own_output, way) for way, j in square]
    grad_pointwise, grad_output = final_call(where, block, pieces, output_pieces)
    return (output[None], grad_frames[None], grad_pointwise, grad_output, small[taps], small[:taps])


def extended_plain(block, sides, width):
    for axis, dim in sides:
        count = lax.axis_size(axis)
        forward = [(i, i + 1) for i in range(count - 1)]
        backward = [(target, source) for source, target in forward]
        low = lax.ppermute(
            lax.slice_in_dim(block, block.shape[dim] - width, None, axis=dim), axis, forward
        )
        high = lax.ppermute(lax.slice_in_dim(block, 0, width, axis=dim), axis, backward)
        block = jnp.concatenate([low, block, high], axis=dim)
    return block


def rounded_term(left, right):
    term = lax.dot_general(
        left, right, (((0,), (0,)), ((), ())), preferred_element_type=jnp.float32
    )
    term = lax.optimization_barrier(term.astype(jnp.bfloat16))
    return term.astype(jnp.float32)


def on_any_mesh(frames, lengths, gain, w_pointwise, w_depthwise, w_output, cotangent):
    frame_count = frames.shape[1]
    width = frames.shape[2]
    taps = w_depthwise.shape[0]
    half_width = (taps - 1) // 2
    full_pointwise, full_output = (
        lax.all_gather(w_pointwise, "fsdp", axis=0, tiled=True),
        lax.all_gather(w_output, "fsdp", axis=0, tiled=True),
    )
    as_float = frames[0].astype(jnp.float32)
    center = jnp.mean(as_float, axis=-1, keepdims=True)
    spread = jnp.mean((as_float - center) ** 2, axis=-1, keepdims=True)
    inverse = lax.rsqrt(spread + EPS)
    normed = (as_float - center) * inverse
    lifted = (normed * gain).astype(jnp.bfloat16)
    position = lax.axis_index("seq") * frame_count + jnp.arange(frame_count, dtype=jnp.int32)
    mask = (position < lengths[0]).astype(jnp.float32)[:, None]
    joined = jnp.dot(lifted, full_pointwise, preferred_element_type=jnp.float32)
    value = joined[:, :width]
    gate_sig = jax.nn.sigmoid(joined[:, width:])
    glu = (value * gate_sig * mask).astype(jnp.bfloat16)
    glu_ext = extended_plain(glu[None], (("seq", 1),), half_width)[0].astype(jnp.float32)
    conv = jnp.zeros((frame_count, width), jnp.float32)
    for offset in range(taps):
        conv = conv + w_depthwise[offset] * glu_ext[offset : offset + frame_count]
    conv_sig = jax.nn.sigmoid(conv)
    swished = (conv * conv_sig).astype(jnp.bfloat16)
    branch = jnp.dot(swished, full_output, preferred_element_type=jnp.float32)
    output = (as_float + branch).astype(jnp.bfloat16)
    branch_grad = (cotangent[0].astype(jnp.float32) * mask).astype(jnp.bfloat16)
    swish_grad = lax.dot_general(
        branch_grad, full_output, (((1,), (1,)), ((), ())), preferred_element_type=jnp.float32
    )
    conv_grad = (swish_grad * conv_sig * (1.0 + conv * (1.0 - conv_sig))).astype(jnp.bfloat16)
    grad_ext = extended_plain(conv_grad[None], (("seq", 1),), half_width)[0].astype(jnp.float32)
    conv_grad_f = conv_grad.astype(jnp.float32)
    glu_grad = jnp.zeros((frame_count, width), jnp.float32)
    tap_rows = []
    for offset in range(taps):
        back = taps - 1 - offset
        glu_grad = glu_grad + w_depthwise[offset] * grad_ext[back : back + frame_count]
        tap_rows.append(jnp.sum(conv_grad_f * glu_ext[offset : offset + frame_count], axis=0))
    glu_grad = glu_grad * mask
    joined_grad = jnp.concatenate(
        [glu_grad * gate_sig, glu_grad * value * gate_sig * (1.0 - gate_sig)], axis=-1
    ).astype(jnp.bfloat16)
    lifted_grad = lax.dot_general(
        joined_grad, full_pointwise, (((1,), (1,)), ((), ())), preferred_element_type=jnp.float32
    )
    gain_term = jnp.sum(lifted_grad * normed, axis=0)
    grad_gain, grad_depthwise = lax.psum((gain_term, jnp.stack(tap_rows, axis=0)), ("seq", "fsdp"))
    scaled = lifted_grad * gain
    norm_grad = inverse * (
        scaled
        - jnp.mean(scaled, axis=-1, keepdims=True)
        - normed * jnp.mean(scaled * normed, axis=-1, keepdims=True)
    )
    grad_frames = (cotangent[0].astype(jnp.float32) + norm_grad).astype(jnp.bfloat16)
    term_pointwise = rounded_term(lifted, joined_grad)
    term_output = rounded_term(swished, branch_grad)
    owned = (
        lax.psum_scatter(
            term_pointwise.astype(jnp.bfloat16), "fsdp", scatter_dimension=0, tiled=True
        ).astype(jnp.float32),
        lax.psum_scatter(
            term_output.astype(jnp.bfloat16), "fsdp", scatter_dimension=0, tiled=True
        ).astype(jnp.float32),
    )
    grad_pointwise, grad_output = (
        lax.psum(owned[0].astype(jnp.bfloat16), "seq").astype(jnp.float32),
        lax.psum(owned[1].astype(jnp.bfloat16), "seq").astype(jnp.float32),
    )
    return (output[None], grad_frames[None], grad_pointwise, grad_output, grad_gain, grad_depthwise)


def solution(mesh):
    in_specs = (
        P("fsdp", "seq", None),
        P("fsdp"),
        P(),
        P("fsdp", None),
        P(),
        P("fsdp", None),
        P("fsdp", "seq", None),
    )
    out_specs = (
        P("fsdp", "seq", None),
        P("fsdp", "seq", None),
        P("fsdp", None),
        P("fsdp", None),
        P(),
        P(),
    )
    known = mesh.shape["seq"] == N_SEQ and mesh.shape["fsdp"] == N_Z * N_CORE
    return jax.shard_map(
        on_slice if known else on_any_mesh,
        mesh=mesh, in_specs=in_specs, out_specs=out_specs, check_vma=False,
    )
```
